512 devices in a mesh: row: 64 (over z_hi, y, x, core), col: 8 (over z_lo).
Axes of the slice: x: 4, y: 4, z: 16 (z_hi: 2, z_lo: 8; z = z_hi * 8 + z_lo), core: 2. Of those that a mesh axis runs over, the one named last changes fastest.
Arguments:
- density: float32 [512, 16, 128, 128], P('row', 'col'), may hold values from -0.75 to 0.75
- columns: int32 [512, 16], P('row', 'col'), may hold values from -1 to 511, as said below
Outputs:
- purified: float32 [512, 16, 128, 128], P('row', 'col')
The draws below stay inside these ranges and needn't reach their ends.
Inputs may be any that keep to these rules, and one draw needn't show every extreme that they name: Block row i lists its occupied block columns in its first slots and -1 in the rest; it has 2 to 16 occupied slots, slot 0 holds column i, the listed columns of a row are distinct, and each listed column j satisfies (j - i) mod 512 <= 8 or (j - i) mod 512 >= 504.
All inputs are finite; a program needn't handle non-finite values.
Results may differ from the reference program's by a relative error of at most 0.0003.
Values sent between devices are 32-bit elements; how exact they have to be, the bound alone decides.
No kernel may reach another device: no remote copies, remote signals or barrier semaphores. Data moves between devices by JAX's collectives and lax.ppermute only.
A program may use at most 128 MiB of HBM per device.

```python
import jax
import jax.numpy as jnp
from jax import lax

B = 128
S = 16
W = 8
NB = 512


def draw_columns(key, part):
    count_key, order_key = jax.random.split(jax.random.fold_in(key, 11))
    counts = jax.random.randint(count_key, (NB,), 2, S + 1).astype(jnp.int32)
    counts = counts.at[0].set(S)
    offsets = jnp.concatenate([jnp.arange(-W, 0), jnp.arange(1, W + 1)]).astype(jnp.int32)
    row_keys = jax.random.split(order_key, NB)
    shuffled = jax.vmap(lambda single: jax.random.permutation(single, offsets))(row_keys)
    chosen = jnp.concatenate([jnp.zeros((NB, 1), jnp.int32), shuffled[:, :S - 1]], axis=1)
    rows = jnp.arange(NB, dtype=jnp.int32)[:, None]
    listed = (rows + chosen) % NB
    slot_ids = jnp.arange(S, dtype=jnp.int32)[None, :]
    return jnp.where(slot_ids < counts[:, None], listed, -1).astype(jnp.int32)


def level_of(key, extent, cuts, smallest, top_value):
    level = 1.0
    for axis_at, parts in cuts:
        heights = jax.random.uniform(jax.random.fold_in(jax.random.fold_in(key, 6), axis_at), (parts,), jnp.float32, smallest / len(cuts), top_value / len(cuts))
        level = level * jnp.repeat(jnp.exp(heights), extent[axis_at] // parts).reshape((-1,) + (1,) * (len(extent) - 1 - axis_at))
    return level


def noise(stream_key, extent, scale, limit, shards=(), kind=jnp.bfloat16):
    loudness = level_of(stream_key, extent, shards, -0.22, 0.18) if shards else 1.0
    entries = jax.random.normal(stream_key, extent, jnp.float32) * scale * loudness
    return jnp.minimum(jnp.maximum(entries, -limit), limit).astype(kind)


def setup_inputs(seed: int = 0) -> dict:
    key_list = jax.random.split(jax.random.key(seed), 3)
    density = noise(key_list[0], (NB, S, B, B), 0.125, 0.75, ((0, 64), (1, 8)), jnp.float32)
    columns = draw_columns(jax.random.fold_in(key_list[2], 71), 0)
    return dict(density=density, columns=columns)


def pattern_product(left, right, columns):
    slots = columns.shape[1]

    def one_row(index):
        own = columns[index]
        safe = jnp.where(own >= 0, own, 0)
        candidate = columns[safe]
        matched = (candidate[None, :, :] == own[:, None, None]) & (own >= 0)[:, None, None] & (own >= 0)[None, :, None]
        weights = matched.astype(jnp.float32)
        chosen = jnp.einsum("sab,abxy->saxy", weights, right[safe], precision=lax.Precision.HIGHEST)
        return jnp.einsum("axk,sakc->sxc", left[index], chosen, precision=lax.Precision.HIGHEST)

    return lax.map(one_row, jnp.arange(columns.shape[0], dtype=jnp.int32))


def reference(density, columns):
    square = pattern_product(density, density, columns)
    cube = pattern_product(square, density, columns)
    return 3.0 * square - 2.0 * cube
```

```python
import jax
import jax.numpy as jnp
from jax import lax
from jax.experimental import pallas as pl
from jax.experimental.pallas import tpu as pltpu
from jax.sharding import Mesh, PartitionSpec as P

W = 8
B = 128
S = 16
ROWS = 8
PANEL = 3 * ROWS
ZERO = PANEL * S
CHUNK = 4
CHUNKS = ROWS * S * (S // CHUNK) + 2
ROW = ("zh", "y", "x", "c")
F32 = jnp.float32
BF16 = jnp.bfloat16


def plan_kernel(where, cols, square_out, square_pairs, cube_out, cube_pairs, counts, table):
    first, place = where[0], where[1]
    count_rows = where[2]

    def clear(k, carry):
        table[k] = -1
        return carry

    lax.fori_loop(0, PANEL * (2 * W + 1), clear, 0)

    def relative(p, b):
        value = cols[p * S + b]
        delta = value - (first - W + p) + count_rows + W
        delta = lax.rem(delta, count_rows)
        return value, p + delta - W

    def block_place(p, b):
        return (p // ROWS) * (ROWS * S) + (b // 2) * (2 * ROWS) + (p % ROWS) * 2 + b % 2

    def fill(k, carry):
        p, b = k // S, k % S
        value, q = relative(p, b)

        @pl.when(value >= 0)
        def _():
            table[p * (2 * W + 1) + q - p + W] = block_place(p, b)

        return carry

    lax.fori_loop(0, PANEL * S, fill, 0)

    def lookup(k, q):
        d = q - k + W
        inside = (d >= 0) & (d <= 2 * W)
        found = table[k * (2 * W + 1) + jnp.clip(d, 0, 2 * W)]
        return jnp.where(inside, found, -1)

    def emit(out_ref, pair_ref, i, s, q, size, at):
        p = W + i

        def term(a, n):
            _, k = relative(p, a)
            found = lookup(k, q)
            entry = at * CHUNK + n

            @pl.when(found >= 0)
            def _():
                pair_ref[2 * entry] = i * S + a
                pair_ref[2 * entry + 1] = found

            return n + (found >= 0).astype(jnp.int32)

        n = lax.fori_loop(0, size, term, 0)
        used = (n + CHUNK - 1) // CHUNK

        def pad(m, carry):
            entry = at * CHUNK + m
            pair_ref[2 * entry] = i * S
            pair_ref[2 * entry + 1] = ZERO
            return carry

        lax.fori_loop(n, used * CHUNK, pad, 0)

        def name(m, carry):
            out_ref[2 * (at + m)] = i * S + s
            out_ref[2 * (at + m) + 1] = (m > 0).astype(jnp.int32)
            return carry

        lax.fori_loop(0, used, name, 0)
        return at + used

    def one_row(i, carry):
        p = W + i

        def occupied(s, n):
            return n + (cols[p * S + s] >= 0).astype(jnp.int32)

        size = lax.fori_loop(0, S, occupied, 0)
        have0 = 2 * place < size
        have1 = 2 * place + 1 < size
        _, q0 = relative(p, 2 * place)
        _, q1 = relative(p, 2 * place + 1)

        def one_slot(s, state):
            at, cube_at = state
            _, q = relative(p, s)
            own = (s // 2) == place
            wanted = own | (have0 & (lookup(q, q0) >= 0)) | (have1 & (lookup(q, q1) >= 0))
            at = lax.cond(
                wanted, lambda: emit(square_out, square_pairs, i, s, q, size, at), lambda: at
            )
            cube_at = lax.cond(
                own, lambda: emit(cube_out, cube_pairs, i, s, q, size, cube_at), lambda: cube_at
            )
            return at, cube_at

        return lax.fori_loop(0, jnp.where(have0, size, 0), one_slot, carry)

    at, cube_at = lax.fori_loop(0, ROWS, one_row, (0, 0))

    def dummy(out_ref, pair_ref, at):
        out_ref[2 * at] = ROWS * S
        out_ref[2 * at + 1] = 0
        for m in range(CHUNK):
            pair_ref[2 * (at * CHUNK + m)] = 0
            pair_ref[2 * (at * CHUNK + m) + 1] = ZERO

    dummy(square_out, square_pairs, at)
    dummy(cube_out, cube_pairs, cube_at)
    counts[0] = (at + 1) // 2
    counts[1] = (cube_at + 1) // 2


def plan(where, cols):
    smem = pl.BlockSpec(memory_space=pltpu.SMEM)
    cube_chunks = ROWS * 2 * (S // CHUNK) + 2
    return pl.pallas_call(
        plan_kernel,
        out_shape=(
            jax.ShapeDtypeStruct((2 * CHUNKS,), jnp.int32),
            jax.ShapeDtypeStruct((2 * CHUNKS * CHUNK,), jnp.int32),
            jax.ShapeDtypeStruct((2 * cube_chunks,), jnp.int32),
            jax.ShapeDtypeStruct((2 * cube_chunks * CHUNK,), jnp.int32),
            jax.ShapeDtypeStruct((2,), jnp.int32),
        ),
        in_specs=[smem, smem],
        out_specs=(smem,) * 5,
        scratch_shapes=[pltpu.SMEM((PANEL * (2 * W + 1),), jnp.int32)],
        name="plan",
    )(where, cols)


def halves(value):
    high = value.astype(BF16)
    return high, (value - high.astype(F32)).astype(BF16)


def product(left, right):
    lh, ll = halves(left)
    rh, rl = halves(right)
    dot = lambda a, b: jnp.dot(a, b, preferred_element_type=F32)
    return dot(lh, rh) + dot(ll, rh) + dot(lh, rl)


def main_kernel(
    where, square_out, square_pairs, cube_out, cube_pairs, counts, cols,
    own, by_x, on_chip, out, panel, square, cube, sems,
):
    place, core, half = where[1], where[3], where[4]
    third = ROWS * S

    def copy(ref, n, to):
        return pltpu.make_async_copy(ref, panel.at[pl.ds(to * third, third)], sems.at[n])

    copies = [
        copy(own.at[half], 0, 1),
        copy(by_x, 1, jnp.where(core == 0, 0, 2)),
        copy(on_chip, 2, jnp.where(core == 0, 2, 0)),
    ]
    for one in copies:
        one.start()
    panel[ZERO] = jnp.zeros((B, B), F32)
    for one in copies:
        one.wait()

    def left_place(code):
        i, a = code // S, code % S
        return third + (a // 2) * (2 * ROWS) + i * 2 + a % 2

    def step(out_ref, pair_ref, load_left, target):
        def body(c, carry):
            for u in range(2):
                at = 2 * c + u
                total = None
                for m in range(CHUNK):
                    entry = 2 * (at * CHUNK + m)
                    term = product(load_left(pair_ref[entry]), panel[pair_ref[entry + 1]])
                    total = term if total is None else total + term
                spot = out_ref[2 * at]
                before = jnp.where(out_ref[2 * at + 1] > 0, target[spot], 0.0)
                target[spot] = before + total
            return carry

        return body

    lax.fori_loop(
        0, counts[0],
        step(square_out, square_pairs, lambda code: panel[left_place(code)], square), 0,
    )
    lax.fori_loop(
        0, counts[1], step(cube_out, cube_pairs, lambda code: square[code], cube), 0
    )

    def finish(k, carry):
        i, s = k // 2, 2 * place + k % 2
        code = i * S + s
        live = cols[(W + i) * S + s] >= 0

        @pl.when(live)
        def _():
            out[k] = 3.0 * square[code] - 2.0 * cube[code]

        @pl.when(jnp.logical_not(live))
        def _():
            out[k] = jnp.zeros((B, B), F32)

        return carry

    lax.fori_loop(0, ROWS * 2, finish, 0)


def compute(where, lists, cols, own, by_x, on_chip):
    hbm = pl.BlockSpec(memory_space=pl.ANY)
    return pl.pallas_call(
        main_kernel,
        out_shape=jax.ShapeDtypeStruct((ROWS * 2, B, B), F32),
        grid_spec=pltpu.PrefetchScalarGridSpec(
            num_scalar_prefetch=7,
            grid=(1,),
            in_specs=[hbm, hbm, hbm],
            out_specs=pl.BlockSpec((ROWS * 2, B, B), lambda i, *_: (0, 0, 0)),
            scratch_shapes=[
                pltpu.VMEM((PANEL * S + 1, B, B), F32),
                pltpu.VMEM((ROWS * S + 1, B, B), F32),
                pltpu.VMEM((ROWS * S + 1, B, B), F32),
                pltpu.SemaphoreType.DMA((3,)),
            ],
        ),
        compiler_params=pltpu.CompilerParams(vmem_limit_bytes=56 << 20),
        cost_estimate=pl.CostEstimate(
            flops=600 * 6 * B ** 3, bytes_accessed=26 << 20, transcendentals=0
        ),
        name="products",
    )(where, *lists, cols, own, by_x, on_chip)


def per_device(density, columns):
    half = lax.axis_index("zh")
    place = lax.axis_index("zl")
    core = lax.axis_index("c")
    local = (lax.axis_index("y") * 4 + lax.axis_index("x")) * 2 + core
    row = half * 32 + local
    raw = density.reshape(ROWS * 2, B, B)
    planes = lax.all_gather(raw, ("zh", "zl"), axis=0, tiled=False)
    planes = planes.reshape(2, ROWS * ROWS * 2, B, B)

    forward = [(i, (i + 1) % 64) for i in range(64)]
    backward = [(b, a) for a, b in forward]
    wide = jnp.concatenate(
        [lax.ppermute(columns, ROW, forward), columns, lax.ppermute(columns, ROW, backward)]
    )
    cols = lax.all_gather(wide, "zl", axis=1, tiled=True).reshape(-1)
    where = jnp.stack([row * ROWS, place, jnp.int32(512), core, half]).astype(jnp.int32)
    lists = plan(where, cols)

    at_end = (local == 0) | (local == 31)
    own_half = lax.dynamic_index_in_dim(planes, half, keepdims=False)
    sent = lax.dynamic_index_in_dim(planes, jnp.where(at_end, 1 - half, half), keepdims=False)
    odd = [(i, (i + 1) % 32) for i in range(1, 32, 2)]
    pairs = [(h * 32 + a, h * 32 + b) for h in range(2) for a, b in odd]
    by_x = lax.ppermute(sent, ROW, pairs + [(b, a) for a, b in pairs])
    on_chip = lax.ppermute(own_half, "c", [(0, 1), (1, 0)])
    result = compute(where, lists, cols, planes, by_x, on_chip)
    return result.reshape(ROWS, 2, B, B)


def solution(mesh):
    fine = Mesh(mesh.devices.reshape(2, 4, 4, 2, 8), ("zh", "y", "x", "c", "zl"))
    return jax.shard_map(
        per_device,
        mesh=fine,
        in_specs=(P(ROW, "zl", None, None), P(ROW, "zl")),
        out_specs=P(ROW, "zl", None, None),
        check_vma=False,
    )
```

```python
import functools

import jax
import jax.numpy as jnp
from jax import lax
from jax.experimental import pallas as pl
from jax.experimental.pallas import tpu as pltpu
from jax.sharding import Mesh, PartitionSpec as P

W = 8
B = 128
S = 16
ROWS = 8
NB = 512
PANEL = 3 * ROWS
BAND = 2 * W + 1
THIRD = ROWS * S
PART = (6, 2)
REACH = [W + 1 + i for i in range(ROWS)]
SENT = (sum(min(S, n) for n in REACH[PART[1]:]), sum(min(S, n) for n in REACH[: PART[1]]))
OWN = (0, PART[0] * S)
CHIP = (THIRD, THIRD + PART[0] * S)
FAR = (2 * THIRD, 2 * THIRD + SENT[0])
ZERO = FAR[1] + SENT[1]
ROW = ("zh", "y", "x", "c")
F32 = jnp.float32
BF16 = jnp.bfloat16
SHAPES = ((4, 2), (4, 2), (2, 4), (4, 2))
CUBE = 3


def list_sizes():
    outs = (ROWS * S,) * 3 + (ROWS * 2,)
    return [n * (S // chunk) + unroll for n, (chunk, unroll) in zip(outs, SHAPES)]


def pick(flag, one, other):
    return jnp.where(flag, one, other)


def in_part(core, i, b):
    second = pick(core == 0, i >= PART[0], i < PART[1])
    inner = pick(second, pick(core == 0, i - PART[0], i), pick(core == 0, i, i - PART[1]))
    return second, (b // 2) * pick(second, 2 * PART[1], 2 * PART[0]) + inner * 2 + b % 2


def plan_kernel(where, cols, send_cols, *refs):
    lists = [refs[2 * n : 2 * n + 2] for n in range(4)]
    counts, sends0, sends1, table = refs[8:]
    first, place, core, send_half, send_first = (where[n] for n in range(5))

    def clear(k, carry):
        table[k] = -1
        return carry

    lax.fori_loop(0, PANEL * BAND, clear, 0)

    def relative(ref, base, p, b):
        value = ref[p * S + b]
        delta = lax.rem(value - (base - W + p) + NB + W, NB)
        return value, p + delta - W

    far_third = 2 * core

    def fill(k, used):
        p, b = k // S, k % S
        value, q = relative(cols, first, p, b)
        third = p // ROWS
        holder = pick(third == 1, core, 1 - core)
        second, inner = in_part(holder, p % ROWS, b)
        far = third == far_third
        reached = (value >= 0) & (q >= 0) & (q < PANEL)
        spot = pick(
            third == 1,
            pick(second, OWN[1], OWN[0]) + inner,
            pick(
                far,
                pick(second, FAR[1] + used[1], FAR[0] + used[0]),
                pick(second, CHIP[1], CHIP[0]) + inner,
            ),
        )

        @pl.when(reached)
        def _():
            table[p * BAND + q - p + W] = spot

        counted = far & reached
        return (
            used[0] + (counted & jnp.logical_not(second)).astype(jnp.int32),
            used[1] + (counted & second).astype(jnp.int32),
        )

    lax.fori_loop(0, PANEL * S, fill, (0, 0))

    low = pick(core == 0, 0, ROWS)
    high = pick(core == 0, 2 * ROWS, PANEL + ROWS)

    def send(k, used):
        i, b = k // S, k % S
        value, q = relative(send_cols, send_first, W + i, b)
        second, inner = in_part(core, i, b)
        go = (value >= 0) & (q >= low) & (q < high)
        go0, go1 = go & jnp.logical_not(second), go & second

        @pl.when(go0)
        def _():
            sends0[used[0]] = send_half * (PART[0] * S) + inner

        @pl.when(go1)
        def _():
            sends1[used[1]] = send_half * (PART[1] * S) + inner

        return used[0] + go0.astype(jnp.int32), used[1] + go1.astype(jnp.int32)

    counts[4], counts[5] = lax.fori_loop(0, ROWS * S, send, (0, 0))

    def lookup(k, q):
        d = q - k + W
        found = table[k * BAND + jnp.clip(d, 0, BAND - 1)]
        return pick((d >= 0) & (d < BAND), found, -1)

    def close(n, which, code, at, seen):
        chunk, _ = SHAPES[which]
        outs, pairs = lists[which]
        used = (n + chunk - 1) // chunk

        def pad(m, carry):
            entry = at * chunk + m
            pairs[2 * entry] = THIRD if which == CUBE else 0
            pairs[2 * entry + 1] = ZERO
            return carry

        lax.fori_loop(n, used * chunk, pad, 0)

        def name(m, carry):
            outs[2 * (at + m)] = code
            outs[2 * (at + m) + 1] = ((m > 0) | seen).astype(jnp.int32)
            return carry

        lax.fori_loop(0, used, name, 0)
        return at + used

    def one_row(i, carry):
        p = W + i

        def occupied(s, n):
            return n + (cols[p * S + s] >= 0).astype(jnp.int32)

        size = lax.fori_loop(0, S, occupied, 0)
        have0 = 2 * place < size
        have1 = 2 * place + 1 < size
        _, q0 = relative(cols, first, p, 2 * place)
        _, q1 = relative(cols, first, p, 2 * place + 1)
        late, _ = in_part(core, i, 0)

        def one_slot(s, state):
            _, q = relative(cols, first, p, s)
            own = (s // 2) == place
            wanted = own | (have0 & (lookup(q, q0) >= 0)) | (have1 & (lookup(q, q1) >= 0))

            def emit():
                def put(which, n, left, right, flag):
                    pairs = lists[which][1]
                    entry = state[which] * SHAPES[which][0] + n

                    @pl.when(flag)
                    def _():
                        pairs[2 * entry] = left
                        pairs[2 * entry + 1] = right

                    return n + flag.astype(jnp.int32)

                def term(a, ns):
                    _, k = relative(cols, first, p, a)
                    found = lookup(k, q)
                    _, inner = in_part(core, i, a)
                    left = pick(late, OWN[1], OWN[0]) + inner
                    live = found >= 0
                    early = (found < OWN[1]) | ((found >= CHIP[0]) & (found < CHIP[1]))
                    now = live & early & jnp.logical_not(late)
                    last = live & (found >= FAR[1])
                    return (
                        put(0, ns[0], left, found, now),
                        put(1, ns[1], left, found, live & jnp.logical_not(now | last)),
                        put(2, ns[2], left, found, last),
                        put(CUBE, ns[3], i * S + a, found, live & own),
                    )

                n0, n1, n2, n3 = lax.fori_loop(0, size, term, (0, 0, 0, 0))
                code = i * S + s
                return (
                    close(n0, 0, code, state[0], False),
                    close(n1, 1, code, state[1], n0 > 0),
                    close(n2, 2, code, state[2], n0 + n1 > 0),
                    close(n3, CUBE, code, state[3], False),
                )

            return lax.cond(wanted, emit, lambda: state)

        return lax.fori_loop(0, pick(have0, size, 0), one_slot, carry)

    ends = lax.fori_loop(0, ROWS, one_row, (0, 0, 0, 0))
    for which, at in enumerate(ends):
        chunk, unroll = SHAPES[which]
        outs, pairs = lists[which]
        for m in range(unroll - 1):
            outs[2 * (at + m)] = THIRD
            outs[2 * (at + m) + 1] = 0
            for n in range(chunk):
                pairs[2 * ((at + m) * chunk + n)] = THIRD if which == CUBE else 0
                pairs[2 * ((at + m) * chunk + n) + 1] = ZERO
        counts[which] = (at + unroll - 1) // unroll


def plan(where, cols, send_cols):
    smem = pl.BlockSpec(memory_space=pltpu.SMEM)
    shapes = []
    for size, (chunk, _) in zip(list_sizes(), SHAPES):
        shapes += [(2 * size,), (2 * size * chunk,)]
    shapes += [(6,), (SENT[0],), (SENT[1],)]
    return pl.pallas_call(
        plan_kernel,
        out_shape=tuple(jax.ShapeDtypeStruct(shape, jnp.int32) for shape in shapes),
        in_specs=[smem] * 3,
        out_specs=(smem,) * len(shapes),
        scratch_shapes=[pltpu.SMEM((PANEL * BAND,), jnp.int32)],
        cost_estimate=pl.CostEstimate(flops=10 ** 10, bytes_accessed=1 << 27, transcendentals=0),
        name="plan",
    )(where, cols, send_cols)


def pack_kernel(which, counts, sends, planes, out, sems):
    def copy(k):
        return pltpu.make_async_copy(planes.at[sends[k]], out.at[k], sems.at[k])

    def start(k, carry):
        copy(k).start()
        return carry

    def wait(k, carry):
        copy(k).wait()
        return carry

    lax.fori_loop(0, counts[4 + which], start, 0)
    lax.fori_loop(0, counts[4 + which], wait, 0)


def pack(which, counts, sends, planes):
    size = SENT[which]
    return pl.pallas_call(
        functools.partial(pack_kernel, which),
        out_shape=jax.ShapeDtypeStruct((size, B, B), F32),
        grid_spec=pltpu.PrefetchScalarGridSpec(
            num_scalar_prefetch=2,
            grid=(1,),
            in_specs=[pl.BlockSpec(memory_space=pl.ANY)],
            out_specs=pl.BlockSpec((size, B, B), lambda i, *_: (0, 0, 0)),
            scratch_shapes=[pltpu.SemaphoreType.DMA((size,))],
        ),
        compiler_params=pltpu.CompilerParams(vmem_limit_bytes=56 << 20),
        cost_estimate=pl.CostEstimate(flops=0, bytes_accessed=10 << 20, transcendentals=0),
        name="pack",
    )(counts, sends, planes)


def halves(value):
    high = value.astype(BF16)
    return high, (value - high.astype(F32)).astype(BF16)


def product(left, right):
    lh, ll = halves(left)
    rh, rl = halves(right)
    dot = lambda a, b: jnp.dot(a, b, preferred_element_type=F32)
    return dot(lh, rh) + dot(ll, rh) + dot(lh, rl)


def run_list(which, outs, pairs, steps, lefts, panel, target, fresh):
    chunk, unroll = SHAPES[which]

    def body(c, carry):
        for u in range(unroll):
            at = unroll * c + u
            total = None
            for m in range(chunk):
                entry = 2 * (at * chunk + m)
                term = product(lefts[pairs[entry]], panel[pairs[entry + 1]])
                total = term if total is None else total + term
            spot = outs[2 * at]
            before = target[spot]
            if fresh:
                before = jnp.where(outs[2 * at + 1] > 0, before, 0.0)
            target[spot] = before + total
        return carry

    lax.fori_loop(0, steps, body, 0)


def start_all(copies):
    for one in copies:
        one.start()


def wait_all(copies):
    for one in copies:
        one.wait()


def part_copies(part, half, planes, on_chip, panel, sems):
    size = PART[part] * S
    return [
        pltpu.make_async_copy(
            source.at[pl.ds(half * size, size)], panel.at[pl.ds(to[part], size)], sems.at[n]
        )
        for n, (source, to) in enumerate(((planes, OWN), (on_chip, CHIP)))
    ]


def whole(source, target, at, size, sem):
    return pltpu.make_async_copy(source, target.at[pl.ds(at, size)], sem)


def give_back(square, square_out, sem):
    back = pltpu.make_async_copy(square.at[pl.ds(0, THIRD)], square_out, sem)
    back.start()
    back.wait()


def first_kernel(where, counts, outs, pairs, planes, on_chip, square_out, panel, square, sems):
    copies = part_copies(0, where[5], planes, on_chip, panel, sems)
    start_all(copies)
    panel[ZERO] = jnp.zeros((B, B), F32)
    wait_all(copies)
    run_list(0, outs, pairs, counts[0], panel, panel, square, True)
    give_back(square, square_out, sems.at[2])


def second_kernel(
    where, counts, outs, pairs, planes0, chip0, planes1, chip1, far0, square_in,
    square_out, panel, square, sems,
):
    copies = part_copies(0, where[5], planes0, chip0, panel, sems)
    copies += part_copies(1, where[5], planes1, chip1, panel, sems.at[pl.ds(2, 2)])
    copies.append(whole(far0, panel, FAR[0], SENT[0], sems.at[4]))
    copies.append(whole(square_in, square, 0, THIRD, sems.at[5]))
    start_all(copies)
    panel[ZERO] = jnp.zeros((B, B), F32)
    wait_all(copies)
    run_list(1, outs, pairs, counts[1], panel, panel, square, True)
    give_back(square, square_out, sems.at[6])


def last_kernel(
    where, counts, outs, pairs, cube_outs, cube_pairs, cols,
    planes0, chip0, planes1, chip1, far0, far1, square_in, out, panel, square, cube, sems,
):
    place = where[1]
    own0, other0 = part_copies(0, where[5], planes0, chip0, panel, sems)
    own1, other1 = part_copies(1, where[5], planes1, chip1, panel, sems.at[pl.ds(2, 2)])
    first = [
        own0, own1, whole(far1, panel, FAR[1], SENT[1], sems.at[5]),
        whole(square_in, square, 0, THIRD, sems.at[6]),
    ]
    later = [other0, other1, whole(far0, panel, FAR[0], SENT[0], sems.at[4])]
    start_all(first)
    start_all(later)
    panel[ZERO] = jnp.zeros((B, B), F32)
    square[THIRD] = jnp.zeros((B, B), F32)
    wait_all(first)
    run_list(2, outs, pairs, counts[2], panel, panel, square, True)
    wait_all(later)
    run_list(CUBE, cube_outs, cube_pairs, counts[CUBE], square, panel, cube, True)

    def finish(k, carry):
        i, s = k // 2, 2 * place + k % 2
        code = i * S + s
        live = cols[(W + i) * S + s] >= 0

        @pl.when(live)
        def _():
            out[k] = 3.0 * square[code] - 2.0 * cube[code]

        @pl.when(jnp.logical_not(live))
        def _():
            out[k] = jnp.zeros((B, B), F32)

        return carry

    lax.fori_loop(0, ROWS * 2, finish, 0)


def call(kernel, scalars, arrays, out_shape, out_spec, scratch, products, name):
    hbm = pl.BlockSpec(memory_space=pl.ANY)
    return pl.pallas_call(
        kernel,
        out_shape=jax.ShapeDtypeStruct(out_shape, F32),
        grid_spec=pltpu.PrefetchScalarGridSpec(
            num_scalar_prefetch=len(scalars),
            grid=(1,),
            in_specs=[hbm] * len(arrays),
            out_specs=out_spec,
            scratch_shapes=scratch,
        ),
        compiler_params=pltpu.CompilerParams(vmem_limit_bytes=56 << 20),
        cost_estimate=pl.CostEstimate(
            flops=products * 6 * B ** 3, bytes_accessed=24 << 20, transcendentals=0
        ),
        name=name,
    )(*scalars, *arrays)


def per_device(density, columns):
    half = lax.axis_index("zh")
    place = lax.axis_index("zl")
    core = lax.axis_index("c")
    local = (lax.axis_index("y") * 4 + lax.axis_index("x")) * 2 + core
    row = half * 32 + local
    starts = (core * PART[1], (1 - core) * PART[0])
    planes = [
        lax.all_gather(
            lax.dynamic_slice_in_dim(density, start, size, axis=0).reshape(size * 2, B, B),
            ("zh", "zl"), axis=0, tiled=True,
        )
        for start, size in zip(starts, PART)
    ]

    forward = [(i, (i + 1) % 64) for i in range(64)]
    backward = [(b, a) for a, b in forward]
    wide = jnp.concatenate(
        [lax.ppermute(columns, ROW, forward), columns, lax.ppermute(columns, ROW, backward)]
    )
    cols = lax.all_gather(wide, "zl", axis=1, tiled=True)
    other_cols = lax.ppermute(cols, "zh", [(0, 1), (1, 0)])
    at_end = (local == 0) | (local == 31)
    send_cols = jnp.where(at_end, other_cols, cols).reshape(-1)
    cols = cols.reshape(-1)
    send_half = jnp.where(at_end, 1 - half, half)
    where = jnp.stack(
        [row * ROWS, place, core, send_half, (send_half * 32 + local) * ROWS, half]
    ).astype(jnp.int32)
    lists = plan(where, cols, send_cols)
    planes[0], lists = lax.optimization_barrier((planes[0], lists))
    list0, list1, list2, list3 = (lists[2 * n : 2 * n + 2] for n in range(4))
    counts, sends0, sends1 = lists[8:]

    inner = [(h * 32 + i, h * 32 + (i + 1) % 32) for h in range(2) for i in range(1, 32, 2)]
    inner += [(b, a) for a, b in inner]
    swap = [(0, 1), (1, 0)]
    panel = pltpu.VMEM((ZERO + 1, B, B), F32)
    blocks = pltpu.VMEM((THIRD + 1, B, B), F32)
    hbm = pl.BlockSpec(memory_space=pl.ANY)

    chip0 = lax.ppermute(planes[0], "c", swap)
    far0 = lax.ppermute(pack(0, counts, sends0, planes[0]), ROW, inner)
    square = call(
        first_kernel, (where, counts, *list0), (planes[0], chip0),
        (THIRD, B, B), hbm, [panel, blocks, pltpu.SemaphoreType.DMA((3,))], 400, "first",
    )
    planes[1], square = lax.optimization_barrier((planes[1], square))
    chip1 = lax.ppermute(planes[1], "c", swap)
    far1 = lax.ppermute(pack(1, counts, sends1, planes[1]), ROW, inner)
    halves_of = (planes[0], chip0, planes[1], chip1)
    square = call(
        second_kernel, (where, counts, *list1), (*halves_of, far0, square),
        (THIRD, B, B), hbm, [panel, blocks, pltpu.SemaphoreType.DMA((7,))], 400, "second",
    )
    result = call(
        last_kernel, (where, counts, *list2, *list3, cols), (*halves_of, far0, far1, square),
        (ROWS * 2, B, B), pl.BlockSpec((ROWS * 2, B, B), lambda i, *_: (0, 0, 0)),
        [panel, blocks, blocks, pltpu.SemaphoreType.DMA((7,))], 200, "last",
    )
    return result.reshape(ROWS, 2, B, B)


def solution(mesh):
    fine = Mesh(mesh.devices.reshape(2, 4, 4, 2, 8), ("zh", "y", "x", "c", "zl"))
    return jax.shard_map(
        per_device,
        mesh=fine,
        in_specs=(P(ROW, "zl", None, None), P(ROW, "zl")),
        out_specs=P(ROW, "zl", None, None),
        check_vma=False,
    )
```

```python
import functools

import jax
import jax.numpy as jnp
from jax import lax
from jax.experimental import pallas as pl
from jax.experimental.pallas import tpu as pltpu
from jax.sharding import Mesh, PartitionSpec as P

W = 8
B = 128
S = 16
ROWS = 8
NB = 512
PANEL = 3 * ROWS
BAND = 2 * W + 1
THIRD = ROWS * S
PART = (7, 1)
REACH = [W + 1 + i for i in range(ROWS)]
SENT = (sum(min(S, n) for n in REACH[PART[1]:]), sum(min(S, n) for n in REACH[: PART[1]]))
OWN = (0, PART[0] * S)
CHIP = (THIRD, THIRD + PART[0] * S)
FAR = (2 * THIRD, 2 * THIRD + SENT[0])
ZERO = FAR[1] + SENT[1]
ROW = ("zh", "y", "x", "c")
F32 = jnp.float32
BF16 = jnp.bfloat16
LIMIT = 34
SHAPES = ((4, 4), (2, 8), (2, 8), (4, 4))
CUBE = 3


def list_sizes():
    outs = (ROWS * S,) * 3 + (ROWS * 2,)
    return [n * (S // chunk) + unroll for n, (chunk, unroll) in zip(outs, SHAPES)]


def pick(flag, one, other):
    return jnp.where(flag, one, other)


def in_part(core, i, b):
    second = pick(core == 0, i >= PART[0], i < PART[1])
    inner = pick(second, pick(core == 0, i - PART[0], i), pick(core == 0, i, i - PART[1]))
    return second, (b // 2) * pick(second, 2 * PART[1], 2 * PART[0]) + inner * 2 + b % 2


def plan_kernel(where, cols, send_cols, *refs):
    lists = [refs[2 * n : 2 * n + 2] for n in range(4)]
    counts, sends0, sends1, table = refs[8:]
    first, place, core, send_half, send_first = (where[n] for n in range(5))

    def clear(k, carry):
        table[k] = -1
        return carry

    lax.fori_loop(0, PANEL * BAND, clear, 0)

    def relative(ref, base, p, b):
        value = ref[p * S + b]
        delta = lax.rem(value - (base - W + p) + NB + W, NB)
        return value, p + delta - W

    far_third = 2 * core

    def fill(k, used):
        p, b = k // S, k % S
        value, q = relative(cols, first, p, b)
        third = p // ROWS
        holder = pick(third == 1, core, 1 - core)
        second, inner = in_part(holder, p % ROWS, b)
        far = third == far_third
        reached = (value >= 0) & (q >= 0) & (q < PANEL)
        spot = pick(
            third == 1,
            pick(second, OWN[1], OWN[0]) + inner,
            pick(
                far,
                pick(second, FAR[1] + used[1], FAR[0] + used[0]),
                pick(second, CHIP[1], CHIP[0]) + inner,
            ),
        )

        @pl.when(reached)
        def _():
            table[p * BAND + q - p + W] = spot

        counted = far & reached
        return (
            used[0] + (counted & jnp.logical_not(second)).astype(jnp.int32),
            used[1] + (counted & second).astype(jnp.int32),
        )

    lax.fori_loop(0, PANEL * S, fill, (0, 0))

    low = pick(core == 0, 0, ROWS)
    high = pick(core == 0, 2 * ROWS, PANEL + ROWS)

    def send(k, used):
        i, b = k // S, k % S
        value, q = relative(send_cols, send_first, W + i, b)
        second, inner = in_part(core, i, b)
        go = (value >= 0) & (q >= low) & (q < high)
        go0, go1 = go & jnp.logical_not(second), go & second

        @pl.when(go0)
        def _():
            sends0[used[0]] = send_half * (PART[0] * S) + inner

        @pl.when(go1)
        def _():
            sends1[used[1]] = send_half * (PART[1] * S) + inner

        return used[0] + go0.astype(jnp.int32), used[1] + go1.astype(jnp.int32)

    counts[4], counts[5] = lax.fori_loop(0, ROWS * S, send, (0, 0))

    def lookup(k, q):
        d = q - k + W
        found = table[k * BAND + jnp.clip(d, 0, BAND - 1)]
        return pick((d >= 0) & (d < BAND), found, -1)

    def close(n, which, code, at, seen):
        chunk, _ = SHAPES[which]
        outs, pairs = lists[which]
        used = (n + chunk - 1) // chunk

        def pad(m, carry):
            entry = at * chunk + m
            pairs[2 * entry] = THIRD if which == CUBE else 0
            pairs[2 * entry + 1] = ZERO
            return carry

        lax.fori_loop(n, used * chunk, pad, 0)

        def name(m, carry):
            outs[2 * (at + m)] = code
            outs[2 * (at + m) + 1] = ((m > 0) | seen).astype(jnp.int32)
            return carry

        lax.fori_loop(0, used, name, 0)
        return at + used

    def one_row(i, carry):
        p = W + i

        def occupied(s, n):
            return n + (cols[p * S + s] >= 0).astype(jnp.int32)

        size = lax.fori_loop(0, S, occupied, 0)
        have0 = 2 * place < size
        have1 = 2 * place + 1 < size
        _, q0 = relative(cols, first, p, 2 * place)
        _, q1 = relative(cols, first, p, 2 * place + 1)
        late, _ = in_part(core, i, 0)

        def one_slot(s, state):
            _, q = relative(cols, first, p, s)
            own = (s // 2) == place
            wanted = own | (have0 & (lookup(q, q0) >= 0)) | (have1 & (lookup(q, q1) >= 0))

            def emit():
                def put(which, n, left, right, flag):
                    pairs = lists[which][1]
                    entry = state[which] * SHAPES[which][0] + n

                    @pl.when(flag)
                    def _():
                        pairs[2 * entry] = left
                        pairs[2 * entry + 1] = right

                    return n + flag.astype(jnp.int32)

                def term(a, ns):
                    _, k = relative(cols, first, p, a)
                    found = lookup(k, q)
                    _, inner = in_part(core, i, a)
                    left = pick(late, OWN[1], OWN[0]) + inner
                    live = found >= 0
                    early = (found < OWN[1]) | ((found >= CHIP[0]) & (found < CHIP[1]))
                    now = live & early & jnp.logical_not(late)
                    last = live & (found >= FAR[0])
                    return (
                        put(0, ns[0], left, found, now),
                        put(1, ns[1], left, found, live & jnp.logical_not(now | last)),
                        put(2, ns[2], left, found, last),
                        put(CUBE, ns[3], i * S + a, found, live & own),
                    )

                n0, n1, n2, n3 = lax.fori_loop(0, size, term, (0, 0, 0, 0))
                code = i * S + s
                return (
                    close(n0, 0, code, state[0], False),
                    close(n1, 1, code, state[1], n0 > 0),
                    close(n2, 2, code, state[2], n0 + n1 > 0),
                    close(n3, CUBE, 2 * i + s % 2, state[3], False),
                )

            return lax.cond(wanted, emit, lambda: state)

        return lax.fori_loop(0, pick(have0, size, 0), one_slot, carry)

    ends = lax.fori_loop(0, ROWS, one_row, (0, 0, 0, 0))
    for which, at in enumerate(ends):
        chunk, unroll = SHAPES[which]
        outs, pairs = lists[which]
        for m in range(unroll - 1):
            outs[2 * (at + m)] = ROWS * 2 if which == CUBE else THIRD
            outs[2 * (at + m) + 1] = 0
            for n in range(chunk):
                pairs[2 * ((at + m) * chunk + n)] = THIRD if which == CUBE else 0
                pairs[2 * ((at + m) * chunk + n) + 1] = ZERO
        counts[which] = (at + unroll - 1) // unroll


def plan(where, cols, send_cols):
    smem = pl.BlockSpec(memory_space=pltpu.SMEM)
    shapes = []
    for size, (chunk, _) in zip(list_sizes(), SHAPES):
        shapes += [(2 * size,), (2 * size * chunk,)]
    shapes += [(6,), (SENT[0],), (SENT[1],)]
    return pl.pallas_call(
        plan_kernel,
        out_shape=tuple(jax.ShapeDtypeStruct(shape, jnp.int32) for shape in shapes),
        in_specs=[smem] * 3,
        out_specs=(smem,) * len(shapes),
        scratch_shapes=[pltpu.SMEM((PANEL * BAND,), jnp.int32)],
        cost_estimate=pl.CostEstimate(flops=10 ** 10, bytes_accessed=1 << 27, transcendentals=0),
        name="plan",
    )(where, cols, send_cols)


def pack_kernel(which, counts, sends, planes, out, sems):
    def copy(k):
        return pltpu.make_async_copy(planes.at[sends[k]], out.at[k], sems.at[k])

    def start(k, carry):
        copy(k).start()
        return carry

    def wait(k, carry):
        copy(k).wait()
        return carry

    lax.fori_loop(0, counts[4 + which], start, 0)
    lax.fori_loop(0, counts[4 + which], wait, 0)


def pack(which, counts, sends, planes):
    size = SENT[which]
    return pl.pallas_call(
        functools.partial(pack_kernel, which),
        out_shape=jax.ShapeDtypeStruct((size, B, B), F32),
        grid_spec=pltpu.PrefetchScalarGridSpec(
            num_scalar_prefetch=2,
            grid=(1,),
            in_specs=[pl.BlockSpec(memory_space=pl.ANY)],
            out_specs=pl.BlockSpec((size, B, B), lambda i, *_: (0, 0, 0)),
            scratch_shapes=[pltpu.SemaphoreType.DMA((size,))],
        ),
        compiler_params=pltpu.CompilerParams(vmem_limit_bytes=56 << 20),
        cost_estimate=pl.CostEstimate(flops=0, bytes_accessed=10 << 20, transcendentals=0),
        name="pack",
    )(counts, sends, planes)


def halves(value):
    high = value.astype(BF16)
    return high, (value - high.astype(F32)).astype(BF16)


def product(left, right):
    lh, ll = halves(left)
    rh, rl = halves(right)
    dot = lambda a, b: jnp.dot(a, b, preferred_element_type=F32)
    return dot(lh, rh) + dot(ll, rh) + dot(lh, rl)


def run_list(which, outs, pairs, steps, lefts, panel, target, fresh):
    chunk, unroll = SHAPES[which]

    def body(c, carry):
        for u in range(unroll):
            at = unroll * c + u
            total = None
            for m in range(chunk):
                entry = 2 * (at * chunk + m)
                term = product(lefts[pairs[entry]], panel[pairs[entry + 1]])
                total = term if total is None else total + term
            spot = outs[2 * at]
            before = target[spot]
            if fresh:
                before = jnp.where(outs[2 * at + 1] > 0, before, 0.0)
            target[spot] = before + total
        return carry

    lax.fori_loop(0, steps, body, 0)


def start_all(copies):
    for one in copies:
        one.start()


def wait_all(copies):
    for one in copies:
        one.wait()


def part_copies(part, half, planes, on_chip, panel, sems):
    size = PART[part] * S
    return [
        pltpu.make_async_copy(
            source.at[pl.ds(half * size, size)], panel.at[pl.ds(to[part], size)], sems.at[n]
        )
        for n, (source, to) in enumerate(((planes, OWN), (on_chip, CHIP)))
    ]


def whole(source, target, at, size, sem):
    return pltpu.make_async_copy(source, target.at[pl.ds(at, size)], sem)


def give_back(square, square_out, sem):
    back = pltpu.make_async_copy(square.at[pl.ds(0, THIRD)], square_out, sem)
    back.start()
    back.wait()


def first_kernel(where, counts, outs, pairs, planes, on_chip, square_out, panel, square, sems):
    copies = part_copies(0, where[5], planes, on_chip, panel, sems)
    start_all(copies)
    panel[ZERO] = jnp.zeros((B, B), F32)
    wait_all(copies)
    run_list(0, outs, pairs, counts[0], panel, panel, square, True)
    give_back(square, square_out, sems.at[2])


def second_kernel(
    where, counts, outs, pairs, planes0, chip0, planes1, chip1, square_in, square_out,
    panel, square, sems,
):
    copies = part_copies(0, where[5], planes0, chip0, panel, sems)
    copies += part_copies(1, where[5], planes1, chip1, panel, sems.at[pl.ds(2, 2)])
    copies.append(whole(square_in, square, 0, THIRD, sems.at[4]))
    start_all(copies)
    panel[ZERO] = jnp.zeros((B, B), F32)
    wait_all(copies)
    run_list(1, outs, pairs, counts[1], panel, panel, square, True)
    give_back(square, square_out, sems.at[5])


def last_kernel(
    where, counts, outs, pairs, cube_outs, cube_pairs, cols,
    planes0, chip0, planes1, chip1, far0, far1, square_in, out, panel, square, cube, sems,
):
    place = where[1]
    own0, other0 = part_copies(0, where[5], planes0, chip0, panel, sems)
    own1, other1 = part_copies(1, where[5], planes1, chip1, panel, sems.at[pl.ds(2, 2)])
    first = [
        own0, own1, whole(far0, panel, FAR[0], SENT[0], sems.at[4]),
        whole(far1, panel, FAR[1], SENT[1], sems.at[5]),
        whole(square_in, square, 0, THIRD, sems.at[6]),
    ]
    later = [other0, other1]
    start_all(first)
    start_all(later)
    panel[ZERO] = jnp.zeros((B, B), F32)
    square[THIRD] = jnp.zeros((B, B), F32)
    wait_all(first)
    run_list(2, outs, pairs, counts[2], panel, panel, square, True)
    wait_all(later)
    run_list(CUBE, cube_outs, cube_pairs, counts[CUBE], square, panel, cube, True)

    def finish(k, carry):
        i, s = k // 2, 2 * place + k % 2
        code = i * S + s
        live = cols[(W + i) * S + s] >= 0

        @pl.when(live)
        def _():
            out[k] = 3.0 * square[code] - 2.0 * cube[k]

        @pl.when(jnp.logical_not(live))
        def _():
            out[k] = jnp.zeros((B, B), F32)

        return carry

    lax.fori_loop(0, ROWS * 2, finish, 0)


def call(kernel, scalars, arrays, out_shape, out_spec, scratch, products, name):
    hbm = pl.BlockSpec(memory_space=pl.ANY)
    return pl.pallas_call(
        kernel,
        out_shape=jax.ShapeDtypeStruct(out_shape, F32),
        grid_spec=pltpu.PrefetchScalarGridSpec(
            num_scalar_prefetch=len(scalars),
            grid=(1,),
            in_specs=[hbm] * len(arrays),
            out_specs=out_spec,
            scratch_shapes=scratch,
        ),
        compiler_params=pltpu.CompilerParams(vmem_limit_bytes=LIMIT << 20),
        cost_estimate=pl.CostEstimate(
            flops=products * 6 * B ** 3, bytes_accessed=24 << 20, transcendentals=0
        ),
        name=name,
    )(*scalars, *arrays)


def per_device(density, columns):
    half = lax.axis_index("zh")
    place = lax.axis_index("zl")
    core = lax.axis_index("c")
    local = (lax.axis_index("y") * 4 + lax.axis_index("x")) * 2 + core
    row = half * 32 + local
    starts = (core * PART[1], (1 - core) * PART[0])
    planes = [
        lax.all_gather(
            lax.dynamic_slice_in_dim(density, start, size, axis=0).reshape(size * 2, B, B),
            ("zh", "zl"), axis=0, tiled=True,
        )
        for start, size in zip(starts, PART)
    ]

    forward = [(i, (i + 1) % 64) for i in range(64)]
    backward = [(b, a) for a, b in forward]
    wide = jnp.concatenate(
        [lax.ppermute(columns, ROW, forward), columns, lax.ppermute(columns, ROW, backward)]
    )
    cols = lax.all_gather(wide, "zl", axis=1, tiled=True)
    other_cols = lax.ppermute(cols, "zh", [(0, 1), (1, 0)])
    at_end = (local == 0) | (local == 31)
    send_cols = jnp.where(at_end, other_cols, cols).reshape(-1)
    cols = cols.reshape(-1)
    send_half = jnp.where(at_end, 1 - half, half)
    where = jnp.stack(
        [row * ROWS, place, core, send_half, (send_half * 32 + local) * ROWS, half]
    ).astype(jnp.int32)
    lists = plan(where, cols, send_cols)
    planes[0], lists = lax.optimization_barrier((planes[0], lists))
    list0, list1, list2, list3 = (lists[2 * n : 2 * n + 2] for n in range(4))
    counts, sends0, sends1 = lists[8:]

    inner = [(h * 32 + i, h * 32 + (i + 1) % 32) for h in range(2) for i in range(1, 32, 2)]
    inner += [(b, a) for a, b in inner]
    swap = [(0, 1), (1, 0)]
    panel = pltpu.VMEM((ZERO + 1, B, B), F32)
    blocks = pltpu.VMEM((THIRD + 1, B, B), F32)
    hbm = pl.BlockSpec(memory_space=pl.ANY)

    chip0 = lax.ppermute(planes[0], "c", swap)
    far0 = lax.ppermute(pack(0, counts, sends0, planes[0]), ROW, inner)
    square = call(
        first_kernel, (where, counts, *list0), (planes[0], chip0),
        (THIRD, B, B), hbm, [panel, blocks, pltpu.SemaphoreType.DMA((3,))], 400, "first",
    )
    planes[1], square = lax.optimization_barrier((planes[1], square))
    far1 = pack(1, counts, sends1, planes[1])
    planes[1], far1 = lax.optimization_barrier((planes[1], far1))
    far1 = lax.ppermute(far1, ROW, inner)
    chip1 = lax.ppermute(planes[1], "c", swap)
    halves_of = (planes[0], chip0, planes[1], chip1)
    square = call(
        second_kernel, (where, counts, *list1), (*halves_of, square),
        (THIRD, B, B), hbm, [panel, blocks, pltpu.SemaphoreType.DMA((7,))], 400, "second",
    )
    result = call(
        last_kernel, (where, counts, *list2, *list3, cols), (*halves_of, far0, far1, square),
        (ROWS * 2, B, B), pl.BlockSpec((ROWS * 2, B, B), lambda i, *_: (0, 0, 0)),
        [panel, blocks, pltpu.VMEM((ROWS * 2 + 1, B, B), F32), pltpu.SemaphoreType.DMA((7,))], 200, "last",
    )
    return result.reshape(ROWS, 2, B, B)


def solution(mesh):
    fine = Mesh(mesh.devices.reshape(2, 4, 4, 2, 8), ("zh", "y", "x", "c", "zl"))
    return jax.shard_map(
        per_device,
        mesh=fine,
        in_specs=(P(ROW, "zl", None, None), P(ROW, "zl")),
        out_specs=P(ROW, "zl", None, None),
        check_vma=False,
    )
```

```python
import functools

import jax
import jax.numpy as jnp
from jax import lax
from jax.experimental import pallas as pl
from jax.experimental.pallas import tpu as pltpu
from jax.sharding import Mesh, PartitionSpec as P

W = 8
B = 128
S = 16
ROWS = 8
NB = 512
PANEL = 3 * ROWS
BAND = 2 * W + 1
THIRD = ROWS * S
PART = (5, 3)
REACH = [W + 1 + i for i in range(ROWS)]
SENT = (sum(min(S, n) for n in REACH[PART[1]:]), sum(min(S, n) for n in REACH[: PART[1]]))
OWN = (0, PART[0] * S)
CHIP = (THIRD, THIRD + PART[0] * S)
FAR = (2 * THIRD, 2 * THIRD + SENT[0])
ZERO = FAR[1] + SENT[1]
ROW = ("zh", "y", "x", "c")
F32 = jnp.float32
BF16 = jnp.bfloat16
LIMIT = 34
SHAPES = ((4, 4), (4, 4), (2, 8), (4, 4))
CUBE = 3


def list_sizes():
    outs = (ROWS * S,) * 3 + (ROWS * 2,)
    return [n * (S // chunk) + unroll for n, (chunk, unroll) in zip(outs, SHAPES)]


def pick(flag, one, other):
    return jnp.where(flag, one, other)


def in_part(core, i, b):
    second = pick(core == 0, i >= PART[0], i < PART[1])
    inner = pick(second, pick(core == 0, i - PART[0], i), pick(core == 0, i, i - PART[1]))
    return second, (b >> 1) * pick(second, 2 * PART[1], 2 * PART[0]) + inner * 2 + (b & 1)


def plan_kernel(where, cols, send_cols, *refs):
    lists = [refs[2 * n : 2 * n + 2] for n in range(4)]
    counts, sends0, sends1, table, row_q, row_left = refs[8:]
    first, place, core, send_half, send_first = (where[n] for n in range(5))

    def clear(k, carry):
        table[k] = -1
        return carry

    lax.fori_loop(0, PANEL * BAND, clear, 0)

    def relative(ref, base, p, b):
        value = ref[p * S + b]
        delta = (value - (base - W + p) + W) & (NB - 1)
        return value, p + delta - W

    far_third = 2 * core

    def fill(k, used):
        p, b = k >> 4, k & (S - 1)
        value, q = relative(cols, first, p, b)
        third = p >> 3
        holder = pick(third == 1, core, 1 - core)
        second, inner = in_part(holder, p & (ROWS - 1), b)
        far = third == far_third
        reached = (value >= 0) & (q >= 0) & (q < PANEL)
        spot = pick(
            third == 1,
            pick(second, OWN[1], OWN[0]) + inner,
            pick(
                far,
                pick(second, FAR[1] + used[1], FAR[0] + used[0]),
                pick(second, CHIP[1], CHIP[0]) + inner,
            ),
        )

        @pl.when(reached)
        def _():
            table[p * BAND + q - p + W] = spot

        counted = far & reached
        return (
            used[0] + (counted & jnp.logical_not(second)).astype(jnp.int32),
            used[1] + (counted & second).astype(jnp.int32),
        )

    lax.fori_loop(0, PANEL * S, fill, (0, 0))

    low = pick(core == 0, 0, ROWS)
    high = pick(core == 0, 2 * ROWS, PANEL + ROWS)

    def send(k, used):
        i, b = k >> 4, k & (S - 1)
        value, q = relative(send_cols, send_first, W + i, b)
        second, inner = in_part(core, i, b)
        go = (value >= 0) & (q >= low) & (q < high)
        go0, go1 = go & jnp.logical_not(second), go & second

        @pl.when(go0)
        def _():
            sends0[used[0]] = send_half * (PART[0] * S) + inner

        @pl.when(go1)
        def _():
            sends1[used[1]] = send_half * (PART[1] * S) + inner

        return used[0] + go0.astype(jnp.int32), used[1] + go1.astype(jnp.int32)

    counts[4], counts[5] = lax.fori_loop(0, ROWS * S, send, (0, 0))

    def lookup(k, q):
        d = q - k + W
        found = table[k * BAND + jnp.clip(d, 0, BAND - 1)]
        return pick((d >= 0) & (d < BAND), found, -1)

    def close(n, which, code, at, seen):
        chunk, _ = SHAPES[which]
        outs, pairs = lists[which]
        used = (n + chunk - 1) >> {2: 1, 4: 2}[chunk]

        def pad(m, carry):
            entry = at * chunk + m
            pairs[2 * entry] = THIRD if which == CUBE else 0
            pairs[2 * entry + 1] = ZERO
            return carry

        lax.fori_loop(n, used * chunk, pad, 0)

        def name(m, carry):
            outs[2 * (at + m)] = code
            outs[2 * (at + m) + 1] = ((m > 0) | seen).astype(jnp.int32)
            return carry

        lax.fori_loop(0, used, name, 0)
        return at + used

    def one_row(i, carry):
        p = W + i

        def occupied(s, n):
            return n + (cols[p * S + s] >= 0).astype(jnp.int32)

        size = lax.fori_loop(0, S, occupied, 0)
        have0 = 2 * place < size
        have1 = 2 * place + 1 < size
        _, q0 = relative(cols, first, p, 2 * place)
        _, q1 = relative(cols, first, p, 2 * place + 1)
        late, _ = in_part(core, i, 0)

        def tabulate(a, carry):
            row_q[a] = relative(cols, first, p, a)[1]
            row_left[a] = pick(late, OWN[1], OWN[0]) + in_part(core, i, a)[1]
            return carry

        lax.fori_loop(0, S, tabulate, 0)

        def one_slot(s, state):
            q = row_q[s]
            own = (s >> 1) == place
            wanted = own | (have0 & (lookup(q, q0) >= 0)) | (have1 & (lookup(q, q1) >= 0))

            def emit():
                def put(which, n, left, right, flag):
                    pairs = lists[which][1]
                    entry = state[which] * SHAPES[which][0] + n

                    @pl.when(flag)
                    def _():
                        pairs[2 * entry] = left
                        pairs[2 * entry + 1] = right

                    return n + flag.astype(jnp.int32)

                def term(a, ns):
                    found = lookup(row_q[a], q)
                    left = row_left[a]
                    live = found >= 0
                    early = (found < OWN[1]) | ((found >= CHIP[0]) & (found < CHIP[1]))
                    now = live & early & jnp.logical_not(late)
                    last = live & (found >= FAR[1])
                    return (
                        put(0, ns[0], left, found, now),
                        put(1, ns[1], left, found, live & jnp.logical_not(now | last)),
                        put(2, ns[2], left, found, last),
                        put(CUBE, ns[3], i * S + a, found, live & own),
                    )

                n0, n1, n2, n3 = lax.fori_loop(0, size, term, (0, 0, 0, 0))
                code = i * S + s
                return (
                    close(n0, 0, code, state[0], False),
                    close(n1, 1, code, state[1], n0 > 0),
                    close(n2, 2, code, state[2], n0 + n1 > 0),
                    close(n3, CUBE, 2 * i + (s & 1), state[3], False),
                )

            return lax.cond(wanted, emit, lambda: state)

        return lax.fori_loop(0, pick(have0, size, 0), one_slot, carry)

    ends = lax.fori_loop(0, ROWS, one_row, (0, 0, 0, 0))
    for which, at in enumerate(ends):
        chunk, unroll = SHAPES[which]
        outs, pairs = lists[which]
        for m in range(unroll - 1):
            outs[2 * (at + m)] = ROWS * 2 if which == CUBE else THIRD
            outs[2 * (at + m) + 1] = 0
            for n in range(chunk):
                pairs[2 * ((at + m) * chunk + n)] = THIRD if which == CUBE else 0
                pairs[2 * ((at + m) * chunk + n) + 1] = ZERO
        counts[which] = (at + unroll - 1) // unroll


def plan(where, cols, send_cols):
    smem = pl.BlockSpec(memory_space=pltpu.SMEM)
    shapes = []
    for size, (chunk, _) in zip(list_sizes(), SHAPES):
        shapes += [(2 * size,), (2 * size * chunk,)]
    shapes += [(6,), (SENT[0],), (SENT[1],)]
    return pl.pallas_call(
        plan_kernel,
        out_shape=tuple(jax.ShapeDtypeStruct(shape, jnp.int32) for shape in shapes),
        in_specs=[smem] * 3,
        out_specs=(smem,) * len(shapes),
        scratch_shapes=[pltpu.SMEM((n,), jnp.int32) for n in (PANEL * BAND, S, S)],
        cost_estimate=pl.CostEstimate(flops=10 ** 10, bytes_accessed=1 << 27, transcendentals=0),
        name="plan",
    )(where, cols, send_cols)


def pack_kernel(which, counts, sends, planes, out, sems):
    def copy(k):
        return pltpu.make_async_copy(planes.at[sends[k]], out.at[k], sems.at[k])

    def start(k, carry):
        copy(k).start()
        return carry

    def wait(k, carry):
        copy(k).wait()
        return carry

    lax.fori_loop(0, counts[4 + which], start, 0)
    lax.fori_loop(0, counts[4 + which], wait, 0)


def pack(which, counts, sends, planes):
    size = SENT[which]
    return pl.pallas_call(
        functools.partial(pack_kernel, which),
        out_shape=jax.ShapeDtypeStruct((size, B, B), F32),
        grid_spec=pltpu.PrefetchScalarGridSpec(
            num_scalar_prefetch=2,
            grid=(1,),
            in_specs=[pl.BlockSpec(memory_space=pl.ANY)],
            out_specs=pl.BlockSpec((size, B, B), lambda i, *_: (0, 0, 0)),
            scratch_shapes=[pltpu.SemaphoreType.DMA((size,))],
        ),
        compiler_params=pltpu.CompilerParams(vmem_limit_bytes=56 << 20),
        cost_estimate=pl.CostEstimate(flops=0, bytes_accessed=10 << 20, transcendentals=0),
        name="pack",
    )(counts, sends, planes)


def halves(value):
    high = value.astype(BF16)
    return high, (value - high.astype(F32)).astype(BF16)


def product(left, right):
    lh, ll = halves(left)
    rh, rl = halves(right)
    dot = lambda a, b: jnp.dot(a, b, preferred_element_type=F32)
    return dot(lh, rh) + dot(ll, rh) + dot(lh, rl)


def run_list(which, outs, pairs, steps, lefts, panel, target, fresh):
    chunk, unroll = SHAPES[which]

    def body(c, carry):
        for u in range(unroll):
            at = unroll * c + u
            total = None
            for m in range(chunk):
                entry = 2 * (at * chunk + m)
                term = product(lefts[pairs[entry]], panel[pairs[entry + 1]])
                total = term if total is None else total + term
            spot = outs[2 * at]
            before = target[spot]
            if fresh:
                before = jnp.where(outs[2 * at + 1] > 0, before, 0.0)
            target[spot] = before + total
        return carry

    lax.fori_loop(0, steps, body, 0)


def start_all(copies):
    for one in copies:
        one.start()


def wait_all(copies):
    for one in copies:
        one.wait()


def part_copies(part, half, planes, on_chip, panel, sems):
    size = PART[part] * S
    return [
        pltpu.make_async_copy(
            source.at[pl.ds(half * size, size)], panel.at[pl.ds(to[part], size)], sems.at[n]
        )
        for n, (source, to) in enumerate(((planes, OWN), (on_chip, CHIP)))
    ]


def whole(source, target, at, size, sem):
    return pltpu.make_async_copy(source, target.at[pl.ds(at, size)], sem)


def give_back(square, square_out, sem):
    back = pltpu.make_async_copy(square.at[pl.ds(0, THIRD)], square_out, sem)
    back.start()
    back.wait()


def first_kernel(where, counts, outs, pairs, planes, on_chip, square_out, panel, square, sems):
    copies = part_copies(0, where[5], planes, on_chip, panel, sems)
    start_all(copies)
    panel[ZERO] = jnp.zeros((B, B), F32)
    wait_all(copies)
    run_list(0, outs, pairs, counts[0], panel, panel, square, True)
    give_back(square, square_out, sems.at[2])


def second_kernel(
    where, counts, outs, pairs, planes0, chip0, planes1, chip1, far0, square_in,
    square_out, panel, square, sems,
):
    copies = part_copies(0, where[5], planes0, chip0, panel, sems)
    copies += part_copies(1, where[5], planes1, chip1, panel, sems.at[pl.ds(2, 2)])
    copies.append(whole(far0, panel, FAR[0], SENT[0], sems.at[4]))
    copies.append(whole(square_in, square, 0, THIRD, sems.at[5]))
    start_all(copies)
    panel[ZERO] = jnp.zeros((B, B), F32)
    wait_all(copies)
    run_list(1, outs, pairs, counts[1], panel, panel, square, True)
    give_back(square, square_out, sems.at[6])


def last_kernel(
    where, counts, outs, pairs, cube_outs, cube_pairs, cols,
    planes0, chip0, planes1, chip1, far0, far1, square_in, out, panel, square, cube, sems,
):
    place = where[1]
    own0, other0 = part_copies(0, where[5], planes0, chip0, panel, sems)
    own1, other1 = part_copies(1, where[5], planes1, chip1, panel, sems.at[pl.ds(2, 2)])
    first = [
        own0, own1, whole(far1, panel, FAR[1], SENT[1], sems.at[5]),
        whole(square_in, square, 0, THIRD, sems.at[6]),
    ]
    later = [other0, other1, whole(far0, panel, FAR[0], SENT[0], sems.at[4])]
    start_all(first)
    start_all(later)
    panel[ZERO] = jnp.zeros((B, B), F32)
    square[THIRD] = jnp.zeros((B, B), F32)
    wait_all(first)
    run_list(2, outs, pairs, counts[2], panel, panel, square, True)
    wait_all(later)
    run_list(CUBE, cube_outs, cube_pairs, counts[CUBE], square, panel, cube, True)

    def finish(k, carry):
        i, s = k // 2, 2 * place + k % 2
        code = i * S + s
        live = cols[(W + i) * S + s] >= 0

        @pl.when(live)
        def _():
            out[k] = 3.0 * square[code] - 2.0 * cube[k]

        @pl.when(jnp.logical_not(live))
        def _():
            out[k] = jnp.zeros((B, B), F32)

        return carry

    lax.fori_loop(0, ROWS * 2, finish, 0)


def call(kernel, scalars, arrays, out_shape, out_spec, scratch, products, name):
    hbm = pl.BlockSpec(memory_space=pl.ANY)
    return pl.pallas_call(
        kernel,
        out_shape=jax.ShapeDtypeStruct(out_shape, F32),
        grid_spec=pltpu.PrefetchScalarGridSpec(
            num_scalar_prefetch=len(scalars),
            grid=(1,),
            in_specs=[hbm] * len(arrays),
            out_specs=out_spec,
            scratch_shapes=scratch,
        ),
        compiler_params=pltpu.CompilerParams(vmem_limit_bytes=LIMIT << 20),
        cost_estimate=pl.CostEstimate(
            flops=products * 6 * B ** 3, bytes_accessed=24 << 20, transcendentals=0
        ),
        name=name,
    )(*scalars, *arrays)


def per_device(density, columns):
    half = lax.axis_index("zh")
    place = lax.axis_index("zl")
    core = lax.axis_index("c")
    local = (lax.axis_index("y") * 4 + lax.axis_index("x")) * 2 + core
    row = half * 32 + local
    starts = (core * PART[1], (1 - core) * PART[0])
    planes = [
        lax.all_gather(
            lax.dynamic_slice_in_dim(density, start, size, axis=0).reshape(size * 2, B, B),
            ("zh", "zl"), axis=0, tiled=True,
        )
        for start, size in zip(starts, PART)
    ]

    forward = [(i, (i + 1) % 64) for i in range(64)]
    backward = [(b, a) for a, b in forward]
    wide = jnp.concatenate(
        [lax.ppermute(columns, ROW, forward), columns, lax.ppermute(columns, ROW, backward)]
    )
    both = lax.all_gather(wide, ("zh", "zl"), axis=1, tiled=True)
    low, high = both[:, :S].reshape(-1), both[:, S:].reshape(-1)
    at_end = (local == 0) | (local == 31)
    cols = jnp.where(half == 0, low, high)
    send_cols = jnp.where((half == 0) ^ at_end, low, high)
    send_half = jnp.where(at_end, 1 - half, half)
    where = jnp.stack(
        [row * ROWS, place, core, send_half, (send_half * 32 + local) * ROWS, half]
    ).astype(jnp.int32)
    lists = plan(where, cols, send_cols)
    planes[0], lists = lax.optimization_barrier((planes[0], lists))
    list0, list1, list2, list3 = (lists[2 * n : 2 * n + 2] for n in range(4))
    counts, sends0, sends1 = lists[8:]

    inner = [(h * 32 + i, h * 32 + (i + 1) % 32) for h in range(2) for i in range(1, 32, 2)]
    inner += [(b, a) for a, b in inner]
    swap = [(0, 1), (1, 0)]
    panel = pltpu.VMEM((ZERO + 1, B, B), F32)
    blocks = pltpu.VMEM((THIRD + 1, B, B), F32)
    hbm = pl.BlockSpec(memory_space=pl.ANY)

    chip0 = lax.ppermute(planes[0], "c", swap)
    far0 = lax.ppermute(pack(0, counts, sends0, planes[0]), ROW, inner)
    square = call(
        first_kernel, (where, counts, *list0), (planes[0], chip0),
        (THIRD, B, B), hbm, [panel, blocks, pltpu.SemaphoreType.DMA((3,))], 400, "first",
    )
    planes[1], square, far0 = lax.optimization_barrier((planes[1], square, far0))
    far1 = pack(1, counts, sends1, planes[1])
    planes[1], far1 = lax.optimization_barrier((planes[1], far1))
    far1 = lax.ppermute(far1, ROW, inner)
    chip1 = lax.ppermute(planes[1], "c", swap)
    halves_of = (planes[0], chip0, planes[1], chip1)
    square = call(
        second_kernel, (where, counts, *list1), (*halves_of, far0, square),
        (THIRD, B, B), hbm, [panel, blocks, pltpu.SemaphoreType.DMA((7,))], 400, "second",
    )
    result = call(
        last_kernel, (where, counts, *list2, *list3, cols), (*halves_of, far0, far1, square),
        (ROWS * 2, B, B), pl.BlockSpec((ROWS * 2, B, B), lambda i, *_: (0, 0, 0)),
        [panel, blocks, pltpu.VMEM((ROWS * 2 + 1, B, B), F32), pltpu.SemaphoreType.DMA((7,))], 200, "last",
    )
    return result.reshape(ROWS, 2, B, B)


def solution(mesh):
    fine = Mesh(mesh.devices.reshape(2, 4, 4, 2, 8), ("zh", "y", "x", "c", "zl"))
    return jax.shard_map(
        per_device,
        mesh=fine,
        in_specs=(P(ROW, "zl", None, None), P(ROW, "zl")),
        out_specs=P(ROW, "zl", None, None),
        check_vma=False,
    )
```

```python
import functools

import jax
import jax.numpy as jnp
from jax import lax
from jax.experimental import pallas as pl
from jax.experimental.pallas import tpu as pltpu
from jax.sharding import Mesh, PartitionSpec as P

W = 8
B = 128
S = 16
ROWS = 8
NB = 512
PANEL = 3 * ROWS
BAND = 2 * W + 1
THIRD = ROWS * S
PART = (5, 3)
REACH = [W + 1 + i for i in range(ROWS)]
SENT = (sum(min(S, n) for n in REACH[PART[1]:]), sum(min(S, n) for n in REACH[: PART[1]]))
OWN = (0, PART[0] * S)
CHIP = (THIRD, THIRD + PART[0] * S)
FAR = (2 * THIRD, 2 * THIRD + SENT[0])
ZERO = FAR[1] + SENT[1]
ROW = ("zh", "y", "x", "c")
F32 = jnp.float32
BF16 = jnp.bfloat16
LIMIT = 34
SHAPES = ((4, 4), (2, 8), (4, 4), (2, 8), (4, 4))
CUBE = 4


def list_sizes():
    outs = (ROWS * S,) * CUBE + (ROWS * 2,)
    return [n * (S // chunk) + unroll for n, (chunk, unroll) in zip(outs, SHAPES)]


def pick(flag, one, other):
    return jnp.where(flag, one, other)


def in_part(core, i, b):
    second = pick(core == 0, i >= PART[0], i < PART[1])
    inner = pick(second, pick(core == 0, i - PART[0], i), pick(core == 0, i, i - PART[1]))
    return second, (b >> 1) * pick(second, 2 * PART[1], 2 * PART[0]) + inner * 2 + (b & 1)


def plan_kernel(where, cols, send_cols, *refs):
    lists = [refs[2 * n : 2 * n + 2] for n in range(5)]
    counts, sends0, sends1, table, row_q, row_left = refs[10:]
    first, place, core, send_half, send_first = (where[n] for n in range(5))

    def clear(k, carry):
        table[k] = -1
        return carry

    lax.fori_loop(0, PANEL * BAND, clear, 0)

    def relative(ref, base, p, b):
        value = ref[p * S + b]
        delta = (value - (base - W + p) + W) & (NB - 1)
        return value, p + delta - W

    far_third = 2 * core

    def fill(k, used):
        p, b = k >> 4, k & (S - 1)
        value, q = relative(cols, first, p, b)
        third = p >> 3
        holder = pick(third == 1, core, 1 - core)
        second, inner = in_part(holder, p & (ROWS - 1), b)
        far = third == far_third
        reached = (value >= 0) & (q >= 0) & (q < PANEL)
        spot = pick(
            third == 1,
            pick(second, OWN[1], OWN[0]) + inner,
            pick(
                far,
                pick(second, FAR[1] + used[1], FAR[0] + used[0]),
                pick(second, CHIP[1], CHIP[0]) + inner,
            ),
        )

        @pl.when(reached)
        def _():
            table[p * BAND + q - p + W] = spot

        counted = far & reached
        return (
            used[0] + (counted & jnp.logical_not(second)).astype(jnp.int32),
            used[1] + (counted & second).astype(jnp.int32),
        )

    lax.fori_loop(0, PANEL * S, fill, (0, 0))

    low = pick(core == 0, 0, ROWS)
    high = pick(core == 0, 2 * ROWS, PANEL + ROWS)

    def send(k, used):
        i, b = k >> 4, k & (S - 1)
        value, q = relative(send_cols, send_first, W + i, b)
        second, inner = in_part(core, i, b)
        go = (value >= 0) & (q >= low) & (q < high)
        go0, go1 = go & jnp.logical_not(second), go & second

        @pl.when(go0)
        def _():
            sends0[used[0]] = send_half * (PART[0] * S) + inner

        @pl.when(go1)
        def _():
            sends1[used[1]] = send_half * (PART[1] * S) + inner

        return used[0] + go0.astype(jnp.int32), used[1] + go1.astype(jnp.int32)

    counts[5], counts[6] = lax.fori_loop(0, ROWS * S, send, (0, 0))

    def lookup(k, q):
        d = q - k + W
        found = table[k * BAND + jnp.clip(d, 0, BAND - 1)]
        return pick((d >= 0) & (d < BAND), found, -1)

    def close(n, which, code, at, seen):
        chunk, _ = SHAPES[which]
        outs, pairs = lists[which]
        used = (n + chunk - 1) >> {2: 1, 4: 2}[chunk]

        def pad(m, carry):
            entry = at * chunk + m
            pairs[2 * entry] = THIRD if which == CUBE else 0
            pairs[2 * entry + 1] = ZERO
            return carry

        lax.fori_loop(n, used * chunk, pad, 0)

        def name(m, carry):
            outs[2 * (at + m)] = code
            outs[2 * (at + m) + 1] = ((m > 0) | seen).astype(jnp.int32)
            return carry

        lax.fori_loop(0, used, name, 0)
        return at + used

    def one_row(i, carry):
        p = W + i

        def occupied(s, n):
            return n + (cols[p * S + s] >= 0).astype(jnp.int32)

        size = lax.fori_loop(0, S, occupied, 0)
        have0 = 2 * place < size
        have1 = 2 * place + 1 < size
        _, q0 = relative(cols, first, p, 2 * place)
        _, q1 = relative(cols, first, p, 2 * place + 1)
        late, _ = in_part(core, i, 0)

        def tabulate(a, carry):
            row_q[a] = relative(cols, first, p, a)[1]
            row_left[a] = pick(late, OWN[1], OWN[0]) + in_part(core, i, a)[1]
            return carry

        lax.fori_loop(0, S, tabulate, 0)

        def one_slot(s, state):
            q = row_q[s]
            own = (s >> 1) == place
            wanted = own | (have0 & (lookup(q, q0) >= 0)) | (have1 & (lookup(q, q1) >= 0))

            def emit():
                def put(which, n, left, right, flag):
                    pairs = lists[which][1]
                    entry = state[which] * SHAPES[which][0] + n

                    @pl.when(flag)
                    def _():
                        pairs[2 * entry] = left
                        pairs[2 * entry + 1] = right

                    return n + flag.astype(jnp.int32)

                def term(a, ns):
                    found = lookup(row_q[a], q)
                    left = row_left[a]
                    live = found >= 0
                    early = (found < OWN[1]) | ((found >= CHIP[0]) & (found < CHIP[1]))
                    now = live & early & jnp.logical_not(late)
                    last = live & (found >= FAR[1])
                    soon = live & (found >= FAR[0]) & jnp.logical_not(last | late)
                    return (
                        put(0, ns[0], left, found, now),
                        put(1, ns[1], left, found, soon),
                        put(2, ns[2], left, found, live & jnp.logical_not(now | soon | last)),
                        put(3, ns[3], left, found, last),
                        put(CUBE, ns[4], i * S + a, found, live & own),
                    )

                n0, n1, n2, n3, n4 = lax.fori_loop(0, size, term, (0,) * 5)
                code = i * S + s
                return (
                    close(n0, 0, code, state[0], False),
                    close(n1, 1, code, state[1], n0 > 0),
                    close(n2, 2, code, state[2], n0 + n1 > 0),
                    close(n3, 3, code, state[3], n0 + n1 + n2 > 0),
                    close(n4, CUBE, 2 * i + (s & 1), state[4], False),
                )

            return lax.cond(wanted, emit, lambda: state)

        return lax.fori_loop(0, pick(have0, size, 0), one_slot, carry)

    ends = lax.fori_loop(0, ROWS, one_row, (0,) * 5)
    for which, at in enumerate(ends):
        chunk, unroll = SHAPES[which]
        outs, pairs = lists[which]
        for m in range(unroll - 1):
            outs[2 * (at + m)] = ROWS * 2 if which == CUBE else THIRD
            outs[2 * (at + m) + 1] = 0
            for n in range(chunk):
                pairs[2 * ((at + m) * chunk + n)] = THIRD if which == CUBE else 0
                pairs[2 * ((at + m) * chunk + n) + 1] = ZERO
        counts[which] = (at + unroll - 1) // unroll


def plan(where, cols, send_cols):
    smem = pl.BlockSpec(memory_space=pltpu.SMEM)
    shapes = []
    for size, (chunk, _) in zip(list_sizes(), SHAPES):
        shapes += [(2 * size,), (2 * size * chunk,)]
    shapes += [(7,), (SENT[0],), (SENT[1],)]
    return pl.pallas_call(
        plan_kernel,
        out_shape=tuple(jax.ShapeDtypeStruct(shape, jnp.int32) for shape in shapes),
        in_specs=[smem] * 3,
        out_specs=(smem,) * len(shapes),
        scratch_shapes=[pltpu.SMEM((n,), jnp.int32) for n in (PANEL * BAND, S, S)],
        cost_estimate=pl.CostEstimate(flops=10 ** 10, bytes_accessed=1 << 27, transcendentals=0),
        name="plan",
    )(where, cols, send_cols)


def pack_kernel(which, counts, sends, planes, out, sems):
    def copy(k):
        return pltpu.make_async_copy(planes.at[sends[k]], out.at[k], sems.at[k])

    def start(k, carry):
        copy(k).start()
        return carry

    def wait(k, carry):
        copy(k).wait()
        return carry

    lax.fori_loop(0, counts[5 + which], start, 0)
    lax.fori_loop(0, counts[5 + which], wait, 0)


def pack(which, counts, sends, planes):
    size = SENT[which]
    return pl.pallas_call(
        functools.partial(pack_kernel, which),
        out_shape=jax.ShapeDtypeStruct((size, B, B), F32),
        grid_spec=pltpu.PrefetchScalarGridSpec(
            num_scalar_prefetch=2,
            grid=(1,),
            in_specs=[pl.BlockSpec(memory_space=pl.ANY)],
            out_specs=pl.BlockSpec((size, B, B), lambda i, *_: (0, 0, 0)),
            scratch_shapes=[pltpu.SemaphoreType.DMA((size,))],
        ),
        compiler_params=pltpu.CompilerParams(vmem_limit_bytes=56 << 20),
        cost_estimate=pl.CostEstimate(flops=0, bytes_accessed=10 << 20, transcendentals=0),
        name="pack",
    )(counts, sends, planes)


def halves(value):
    high = value.astype(BF16)
    return high, (value - high.astype(F32)).astype(BF16)


def product(left, right):
    lh, ll = halves(left)
    rh, rl = halves(right)
    dot = lambda a, b: jnp.dot(a, b, preferred_element_type=F32)
    return dot(lh, rh) + dot(ll, rh) + dot(lh, rl)


def run_list(which, outs, pairs, steps, lefts, panel, target, fresh):
    chunk, unroll = SHAPES[which]

    def body(c, carry):
        for u in range(unroll):
            at = unroll * c + u
            total = None
            for m in range(chunk):
                entry = 2 * (at * chunk + m)
                term = product(lefts[pairs[entry]], panel[pairs[entry + 1]])
                total = term if total is None else total + term
            spot = outs[2 * at]
            before = target[spot]
            if fresh:
                before = jnp.where(outs[2 * at + 1] > 0, before, 0.0)
            target[spot] = before + total
        return carry

    lax.fori_loop(0, steps, body, 0)


def start_all(copies):
    for one in copies:
        one.start()


def wait_all(copies):
    for one in copies:
        one.wait()


def part_copies(part, half, planes, on_chip, panel, sems):
    size = PART[part] * S
    return [
        pltpu.make_async_copy(
            source.at[pl.ds(half * size, size)], panel.at[pl.ds(to[part], size)], sems.at[n]
        )
        for n, (source, to) in enumerate(((planes, OWN), (on_chip, CHIP)))
    ]


def whole(source, target, at, size, sem):
    return pltpu.make_async_copy(source, target.at[pl.ds(at, size)], sem)


def give_back(square, square_out, sem):
    back = pltpu.make_async_copy(square.at[pl.ds(0, THIRD)], square_out, sem)
    back.start()
    back.wait()


def first_kernel(where, counts, outs, pairs, planes, on_chip, square_out, panel, square, sems):
    copies = part_copies(0, where[5], planes, on_chip, panel, sems)
    start_all(copies)
    panel[ZERO] = jnp.zeros((B, B), F32)
    wait_all(copies)
    run_list(0, outs, pairs, counts[0], panel, panel, square, True)
    give_back(square, square_out, sems.at[2])


def early_kernel(
    where, counts, outs, pairs, planes0, far0, square_in, square_out, panel, square, sems
):
    size = PART[0] * S
    own = planes0.at[pl.ds(where[5] * size, size)]
    copies = [
        whole(own, panel, OWN[0], size, sems.at[0]),
        whole(far0, panel, FAR[0], SENT[0], sems.at[1]),
        whole(square_in, square, 0, THIRD, sems.at[2]),
    ]
    start_all(copies)
    panel[ZERO] = jnp.zeros((B, B), F32)
    wait_all(copies)
    run_list(1, outs, pairs, counts[1], panel, panel, square, True)
    give_back(square, square_out, sems.at[3])


def second_kernel(
    where, counts, outs, pairs, planes0, chip0, planes1, chip1, far0, square_in,
    square_out, panel, square, sems,
):
    copies = part_copies(0, where[5], planes0, chip0, panel, sems)
    copies += part_copies(1, where[5], planes1, chip1, panel, sems.at[pl.ds(2, 2)])
    copies.append(whole(far0, panel, FAR[0], SENT[0], sems.at[4]))
    copies.append(whole(square_in, square, 0, THIRD, sems.at[5]))
    start_all(copies)
    panel[ZERO] = jnp.zeros((B, B), F32)
    wait_all(copies)
    run_list(2, outs, pairs, counts[2], panel, panel, square, True)
    give_back(square, square_out, sems.at[6])


def last_kernel(
    where, counts, outs, pairs, cube_outs, cube_pairs, cols,
    planes0, chip0, planes1, chip1, far0, far1, square_in, out, panel, square, cube, sems,
):
    place = where[1]
    own0, other0 = part_copies(0, where[5], planes0, chip0, panel, sems)
    own1, other1 = part_copies(1, where[5], planes1, chip1, panel, sems.at[pl.ds(2, 2)])
    first = [
        own0, own1, whole(far1, panel, FAR[1], SENT[1], sems.at[5]),
        whole(square_in, square, 0, THIRD, sems.at[6]),
    ]
    later = [other0, other1, whole(far0, panel, FAR[0], SENT[0], sems.at[4])]
    start_all(first)
    start_all(later)
    panel[ZERO] = jnp.zeros((B, B), F32)
    square[THIRD] = jnp.zeros((B, B), F32)
    wait_all(first)
    run_list(3, outs, pairs, counts[3], panel, panel, square, True)
    wait_all(later)
    run_list(CUBE, cube_outs, cube_pairs, counts[CUBE], square, panel, cube, True)

    def finish(k, carry):
        i, s = k // 2, 2 * place + k % 2
        code = i * S + s
        live = cols[(W + i) * S + s] >= 0

        @pl.when(live)
        def _():
            out[k] = 3.0 * square[code] - 2.0 * cube[k]

        @pl.when(jnp.logical_not(live))
        def _():
            out[k] = jnp.zeros((B, B), F32)

        return carry

    lax.fori_loop(0, ROWS * 2, finish, 0)


def call(kernel, scalars, arrays, out_shape, out_spec, scratch, products, name):
    hbm = pl.BlockSpec(memory_space=pl.ANY)
    return pl.pallas_call(
        kernel,
        out_shape=jax.ShapeDtypeStruct(out_shape, F32),
        grid_spec=pltpu.PrefetchScalarGridSpec(
            num_scalar_prefetch=len(scalars),
            grid=(1,),
            in_specs=[hbm] * len(arrays),
            out_specs=out_spec,
            scratch_shapes=scratch,
        ),
        compiler_params=pltpu.CompilerParams(vmem_limit_bytes=LIMIT << 20),
        cost_estimate=pl.CostEstimate(
            flops=products * 6 * B ** 3, bytes_accessed=24 << 20, transcendentals=0
        ),
        name=name,
    )(*scalars, *arrays)


def per_device(density, columns):
    half = lax.axis_index("zh")
    place = lax.axis_index("zl")
    core = lax.axis_index("c")
    local = (lax.axis_index("y") * 4 + lax.axis_index("x")) * 2 + core
    row = half * 32 + local
    starts = (core * PART[1], (1 - core) * PART[0])
    planes = [
        lax.all_gather(
            lax.dynamic_slice_in_dim(density, start, size, axis=0).reshape(size * 2, B, B),
            ("zh", "zl"), axis=0, tiled=True,
        )
        for start, size in zip(starts, PART)
    ]

    forward = [(i, (i + 1) % 64) for i in range(64)]
    backward = [(b, a) for a, b in forward]
    wide = jnp.concatenate(
        [lax.ppermute(columns, ROW, forward), columns, lax.ppermute(columns, ROW, backward)]
    )
    both = lax.all_gather(wide, ("zh", "zl"), axis=1, tiled=True)
    low, high = both[:, :S].reshape(-1), both[:, S:].reshape(-1)
    at_end = (local == 0) | (local == 31)
    cols = jnp.where(half == 0, low, high)
    send_cols = jnp.where((half == 0) ^ at_end, low, high)
    send_half = jnp.where(at_end, 1 - half, half)
    where = jnp.stack(
        [row * ROWS, place, core, send_half, (send_half * 32 + local) * ROWS, half]
    ).astype(jnp.int32)
    lists = plan(where, cols, send_cols)
    planes[0], lists = lax.optimization_barrier((planes[0], lists))
    list0, list1, list2, list3, list4 = (lists[2 * n : 2 * n + 2] for n in range(5))
    counts, sends0, sends1 = lists[10:]

    inner = [(h * 32 + i, h * 32 + (i + 1) % 32) for h in range(2) for i in range(1, 32, 2)]
    inner += [(b, a) for a, b in inner]
    swap = [(0, 1), (1, 0)]
    panel = pltpu.VMEM((ZERO + 1, B, B), F32)
    blocks = pltpu.VMEM((THIRD + 1, B, B), F32)
    hbm = pl.BlockSpec(memory_space=pl.ANY)

    chip0 = lax.ppermute(planes[0], "c", swap)
    far0 = lax.ppermute(pack(0, counts, sends0, planes[0]), ROW, inner)
    square = call(
        first_kernel, (where, counts, *list0), (planes[0], chip0),
        (THIRD, B, B), hbm, [panel, blocks, pltpu.SemaphoreType.DMA((3,))], 400, "first",
    )
    square = call(
        early_kernel, (where, counts, *list1), (planes[0], far0, square),
        (THIRD, B, B), hbm, [panel, blocks, pltpu.SemaphoreType.DMA((4,))], 100, "early",
    )
    planes[1], square = lax.optimization_barrier((planes[1], square))
    chip1 = lax.ppermute(planes[1], "c", swap)
    far1 = lax.ppermute(pack(1, counts, sends1, planes[1]), ROW, inner)
    halves_of = (planes[0], chip0, planes[1], chip1)
    square = call(
        second_kernel, (where, counts, *list2), (*halves_of, far0, square),
        (THIRD, B, B), hbm, [panel, blocks, pltpu.SemaphoreType.DMA((7,))], 400, "second",
    )
    result = call(
        last_kernel, (where, counts, *list3, *list4, cols), (*halves_of, far0, far1, square),
        (ROWS * 2, B, B), pl.BlockSpec((ROWS * 2, B, B), lambda i, *_: (0, 0, 0)),
        [panel, blocks, pltpu.VMEM((ROWS * 2 + 1, B, B), F32), pltpu.SemaphoreType.DMA((7,))], 200, "last",
    )
    return result.reshape(ROWS, 2, B, B)


def solution(mesh):
    fine = Mesh(mesh.devices.reshape(2, 4, 4, 2, 8), ("zh", "y", "x", "c", "zl"))
    return jax.shard_map(
        per_device,
        mesh=fine,
        in_specs=(P(ROW, "zl", None, None), P(ROW, "zl")),
        out_specs=P(ROW, "zl", None, None),
        check_vma=False,
    )
```

```python
import functools

import jax
import jax.numpy as jnp
from jax import lax
from jax.experimental import pallas as pl
from jax.experimental.pallas import tpu as pltpu
from jax.sharding import Mesh, PartitionSpec as P

W = 8
B = 128
S = 16
ROWS = 8
NB = 512
PANEL = 3 * ROWS
BAND = 2 * W + 1
THIRD = ROWS * S
PART = (5, 3)
REACH = [W + 1 + i for i in range(ROWS)]
SENT = (sum(min(S, n) for n in REACH[PART[1]:]), sum(min(S, n) for n in REACH[: PART[1]]))
OWN = (0, PART[0] * S)
CHIP = (THIRD, THIRD + PART[0] * S)
FAR = (2 * THIRD, 2 * THIRD + SENT[0])
ZERO = FAR[1] + SENT[1]
ROW = ("zh", "y", "x", "c")
F32 = jnp.float32
BF16 = jnp.bfloat16
LIMIT = 34
SHAPES = ((2, 8), (2, 8), (2, 8), (2, 8), (4, 4))
CUBE = 4


def list_sizes():
    outs = (ROWS * S,) * CUBE + (ROWS * 2,)
    return [n * (S // chunk) + unroll for n, (chunk, unroll) in zip(outs, SHAPES)]


def pick(flag, one, other):
    return jnp.where(flag, one, other)


def in_part(core, i, b):
    second = pick(core == 0, i >= PART[0], i < PART[1])
    inner = pick(second, pick(core == 0, i - PART[0], i), pick(core == 0, i, i - PART[1]))
    return second, (b >> 1) * pick(second, 2 * PART[1], 2 * PART[0]) + inner * 2 + (b & 1)


def plan_kernel(where, cols, send_cols, *refs):
    lists = [refs[2 * n : 2 * n + 2] for n in range(5)]
    counts, sends0, sends1, table, row_q, row_left = refs[10:]
    first, place, core, send_half, send_first = (where[n] for n in range(5))

    def clear(k, carry):
        table[k] = -1
        return carry

    lax.fori_loop(0, PANEL * BAND, clear, 0)

    def relative(ref, base, p, b):
        value = ref[p * S + b]
        delta = (value - (base - W + p) + W) & (NB - 1)
        return value, p + delta - W

    far_third = 2 * core

    def fill(k, used):
        p, b = k >> 4, k & (S - 1)
        value, q = relative(cols, first, p, b)
        third = p >> 3
        holder = pick(third == 1, core, 1 - core)
        second, inner = in_part(holder, p & (ROWS - 1), b)
        far = third == far_third
        reached = (value >= 0) & (q >= 0) & (q < PANEL)
        spot = pick(
            third == 1,
            pick(second, OWN[1], OWN[0]) + inner,
            pick(
                far,
                pick(second, FAR[1] + used[1], FAR[0] + used[0]),
                pick(second, CHIP[1], CHIP[0]) + inner,
            ),
        )

        @pl.when(reached)
        def _():
            table[p * BAND + q - p + W] = spot

        counted = far & reached
        return (
            used[0] + (counted & jnp.logical_not(second)).astype(jnp.int32),
            used[1] + (counted & second).astype(jnp.int32),
        )

    lax.fori_loop(0, PANEL * S, fill, (0, 0))

    low = pick(core == 0, 0, ROWS)
    high = pick(core == 0, 2 * ROWS, PANEL + ROWS)

    def send(k, used):
        i, b = k >> 4, k & (S - 1)
        value, q = relative(send_cols, send_first, W + i, b)
        second, inner = in_part(core, i, b)
        go = (value >= 0) & (q >= low) & (q < high)
        go0, go1 = go & jnp.logical_not(second), go & second

        @pl.when(go0)
        def _():
            sends0[used[0]] = send_half * (PART[0] * S) + inner

        @pl.when(go1)
        def _():
            sends1[used[1]] = send_half * (PART[1] * S) + inner

        return used[0] + go0.astype(jnp.int32), used[1] + go1.astype(jnp.int32)

    counts[5], counts[6] = lax.fori_loop(0, ROWS * S, send, (0, 0))

    def lookup(k, q):
        d = q - k + W
        found = table[k * BAND + jnp.clip(d, 0, BAND - 1)]
        return pick((d >= 0) & (d < BAND), found, -1)

    def close(n, which, code, at, seen):
        chunk, _ = SHAPES[which]
        outs, pairs = lists[which]
        used = (n + chunk - 1) >> {2: 1, 4: 2}[chunk]

        def pad(m, carry):
            entry = at * chunk + m
            pairs[2 * entry] = THIRD if which == CUBE else 0
            pairs[2 * entry + 1] = ZERO
            return carry

        lax.fori_loop(n, used * chunk, pad, 0)

        def name(m, carry):
            outs[2 * (at + m)] = code
            outs[2 * (at + m) + 1] = ((m > 0) | seen).astype(jnp.int32)
            return carry

        lax.fori_loop(0, used, name, 0)
        return at + used

    def one_row(i, carry):
        p = W + i

        def occupied(s, n):
            return n + (cols[p * S + s] >= 0).astype(jnp.int32)

        size = lax.fori_loop(0, S, occupied, 0)
        have0 = 2 * place < size
        have1 = 2 * place + 1 < size
        _, q0 = relative(cols, first, p, 2 * place)
        _, q1 = relative(cols, first, p, 2 * place + 1)
        late, _ = in_part(core, i, 0)

        def tabulate(a, carry):
            row_q[a] = relative(cols, first, p, a)[1]
            row_left[a] = pick(late, OWN[1], OWN[0]) + in_part(core, i, a)[1]
            return carry

        lax.fori_loop(0, S, tabulate, 0)

        def one_slot(s, state):
            q = row_q[s]
            own = (s >> 1) == place
            wanted = own | (have0 & (lookup(q, q0) >= 0)) | (have1 & (lookup(q, q1) >= 0))

            def emit():
                def put(which, n, left, right, flag):
                    pairs = lists[which][1]
                    entry = state[which] * SHAPES[which][0] + n

                    @pl.when(flag)
                    def _():
                        pairs[2 * entry] = left
                        pairs[2 * entry + 1] = right

                    return n + flag.astype(jnp.int32)

                def term(a, ns):
                    found = lookup(row_q[a], q)
                    left = row_left[a]
                    live = found >= 0
                    early = (found < OWN[1]) | ((found >= CHIP[0]) & (found < CHIP[1]))
                    now = live & early & jnp.logical_not(late)
                    last = live & (found >= FAR[1])
                    soon = live & (found >= FAR[0]) & jnp.logical_not(last | late)
                    return (
                        put(0, ns[0], left, found, now),
                        put(1, ns[1], left, found, soon),
                        put(2, ns[2], left, found, live & jnp.logical_not(now | soon | last)),
                        put(3, ns[3], left, found, last),
                        put(CUBE, ns[4], i * S + a, found, live & own),
                    )

                n0, n1, n2, n3, n4 = lax.fori_loop(0, size, term, (0,) * 5)
                code = i * S + s
                return (
                    close(n0, 0, code, state[0], False),
                    close(n1, 1, code, state[1], n0 > 0),
                    close(n2, 2, code, state[2], n0 + n1 > 0),
                    close(n3, 3, code, state[3], n0 + n1 + n2 > 0),
                    close(n4, CUBE, 2 * i + (s & 1), state[4], False),
                )

            return lax.cond(wanted, emit, lambda: state)

        return lax.fori_loop(0, pick(have0, size, 0), one_slot, carry)

    ends = lax.fori_loop(0, ROWS, one_row, (0,) * 5)
    for which, at in enumerate(ends):
        chunk, unroll = SHAPES[which]
        outs, pairs = lists[which]
        for m in range(unroll - 1):
            outs[2 * (at + m)] = ROWS * 2 if which == CUBE else THIRD
            outs[2 * (at + m) + 1] = 0
            for n in range(chunk):
                pairs[2 * ((at + m) * chunk + n)] = THIRD if which == CUBE else 0
                pairs[2 * ((at + m) * chunk + n) + 1] = ZERO
        counts[which] = (at + unroll - 1) // unroll


def plan(where, cols, send_cols):
    smem = pl.BlockSpec(memory_space=pltpu.SMEM)
    shapes = []
    for size, (chunk, _) in zip(list_sizes(), SHAPES):
        shapes += [(2 * size,), (2 * size * chunk,)]
    shapes += [(7,), (SENT[0],), (SENT[1],)]
    return pl.pallas_call(
        plan_kernel,
        out_shape=tuple(jax.ShapeDtypeStruct(shape, jnp.int32) for shape in shapes),
        in_specs=[smem] * 3,
        out_specs=(smem,) * len(shapes),
        scratch_shapes=[pltpu.SMEM((n,), jnp.int32) for n in (PANEL * BAND, S, S)],
        cost_estimate=pl.CostEstimate(flops=10 ** 10, bytes_accessed=1 << 27, transcendentals=0),
        name="plan",
    )(where, cols, send_cols)


def pack_kernel(which, counts, sends, planes, out, sems):
    def copy(k):
        return pltpu.make_async_copy(planes.at[sends[k]], out.at[k], sems.at[k])

    def start(k, carry):
        copy(k).start()
        return carry

    def wait(k, carry):
        copy(k).wait()
        return carry

    lax.fori_loop(0, counts[5 + which], start, 0)
    lax.fori_loop(0, counts[5 + which], wait, 0)


def pack(which, counts, sends, planes):
    size = SENT[which]
    return pl.pallas_call(
        functools.partial(pack_kernel, which),
        out_shape=jax.ShapeDtypeStruct((size, B, B), F32),
        grid_spec=pltpu.PrefetchScalarGridSpec(
            num_scalar_prefetch=2,
            grid=(1,),
            in_specs=[pl.BlockSpec(memory_space=pl.ANY)],
            out_specs=pl.BlockSpec((size, B, B), lambda i, *_: (0, 0, 0)),
            scratch_shapes=[pltpu.SemaphoreType.DMA((size,))],
        ),
        compiler_params=pltpu.CompilerParams(vmem_limit_bytes=56 << 20),
        cost_estimate=pl.CostEstimate(flops=0, bytes_accessed=10 << 20, transcendentals=0),
        name="pack",
    )(counts, sends, planes)


def halves(value):
    high = value.astype(BF16)
    return high, (value - high.astype(F32)).astype(BF16)


def product(left, right):
    lh, ll = halves(left)
    rh, rl = halves(right)
    dot = lambda a, b: jnp.dot(a, b, preferred_element_type=F32)
    return dot(lh, rh) + dot(ll, rh) + dot(lh, rl)


def run_list(which, outs, pairs, steps, lefts, panel, target, fresh):
    chunk, unroll = SHAPES[which]

    def body(c, carry):
        for u in range(unroll):
            at = unroll * c + u
            total = None
            for m in range(chunk):
                entry = 2 * (at * chunk + m)
                term = product(lefts[pairs[entry]], panel[pairs[entry + 1]])
                total = term if total is None else total + term
            spot = outs[2 * at]
            before = target[spot]
            if fresh:
                before = jnp.where(outs[2 * at + 1] > 0, before, 0.0)
            target[spot] = before + total
        return carry

    lax.fori_loop(0, steps, body, 0)


def start_all(copies):
    for one in copies:
        one.start()


def wait_all(copies):
    for one in copies:
        one.wait()


def part_copies(part, half, planes, on_chip, panel, sems):
    size = PART[part] * S
    return [
        pltpu.make_async_copy(
            source.at[pl.ds(half * size, size)], panel.at[pl.ds(to[part], size)], sems.at[n]
        )
        for n, (source, to) in enumerate(((planes, OWN), (on_chip, CHIP)))
    ]


def whole(source, target, at, size, sem):
    return pltpu.make_async_copy(source, target.at[pl.ds(at, size)], sem)


def give_back(square, square_out, sem):
    back = pltpu.make_async_copy(square.at[pl.ds(0, THIRD)], square_out, sem)
    back.start()
    back.wait()


def first_kernel(where, counts, outs, pairs, planes, on_chip, square_out, panel, square, sems):
    copies = part_copies(0, where[5], planes, on_chip, panel, sems)
    start_all(copies)
    panel[ZERO] = jnp.zeros((B, B), F32)
    wait_all(copies)
    run_list(0, outs, pairs, counts[0], panel, panel, square, True)
    give_back(square, square_out, sems.at[2])


def early_kernel(
    where, counts, outs, pairs, planes0, far0, square_in, square_out, panel, square, sems
):
    size = PART[0] * S
    own = planes0.at[pl.ds(where[5] * size, size)]
    copies = [
        whole(own, panel, OWN[0], size, sems.at[0]),
        whole(far0, panel, FAR[0], SENT[0], sems.at[1]),
        whole(square_in, square, 0, THIRD, sems.at[2]),
    ]
    start_all(copies)
    panel[ZERO] = jnp.zeros((B, B), F32)
    wait_all(copies)
    run_list(1, outs, pairs, counts[1], panel, panel, square, True)
    give_back(square, square_out, sems.at[3])


def second_kernel(
    where, counts, outs, pairs, planes0, chip0, planes1, chip1, far0, square_in,
    square_out, panel, square, sems,
):
    copies = part_copies(0, where[5], planes0, chip0, panel, sems)
    copies += part_copies(1, where[5], planes1, chip1, panel, sems.at[pl.ds(2, 2)])
    copies.append(whole(far0, panel, FAR[0], SENT[0], sems.at[4]))
    copies.append(whole(square_in, square, 0, THIRD, sems.at[5]))
    start_all(copies)
    panel[ZERO] = jnp.zeros((B, B), F32)
    wait_all(copies)
    run_list(2, outs, pairs, counts[2], panel, panel, square, True)
    give_back(square, square_out, sems.at[6])


def last_kernel(
    where, counts, outs, pairs, cube_outs, cube_pairs, cols,
    planes0, chip0, planes1, chip1, far0, far1, square_in, out, panel, square, cube, sems,
):
    place = where[1]
    own0, other0 = part_copies(0, where[5], planes0, chip0, panel, sems)
    own1, other1 = part_copies(1, where[5], planes1, chip1, panel, sems.at[pl.ds(2, 2)])
    first = [
        own0, own1, whole(far1, panel, FAR[1], SENT[1], sems.at[5]),
        whole(square_in, square, 0, THIRD, sems.at[6]),
    ]
    later = [other0, other1, whole(far0, panel, FAR[0], SENT[0], sems.at[4])]
    start_all(first)
    start_all(later)
    panel[ZERO] = jnp.zeros((B, B), F32)
    square[THIRD] = jnp.zeros((B, B), F32)
    wait_all(first)
    run_list(3, outs, pairs, counts[3], panel, panel, square, True)
    wait_all(later)
    run_list(CUBE, cube_outs, cube_pairs, counts[CUBE], square, panel, cube, True)

    def finish(k, carry):
        i, s = k // 2, 2 * place + k % 2
        code = i * S + s
        live = cols[(W + i) * S + s] >= 0

        @pl.when(live)
        def _():
            out[k] = 3.0 * square[code] - 2.0 * cube[k]

        @pl.when(jnp.logical_not(live))
        def _():
            out[k] = jnp.zeros((B, B), F32)

        return carry

    lax.fori_loop(0, ROWS * 2, finish, 0)


def call(kernel, scalars, arrays, out_shape, out_spec, scratch, products, name):
    hbm = pl.BlockSpec(memory_space=pl.ANY)
    return pl.pallas_call(
        kernel,
        out_shape=jax.ShapeDtypeStruct(out_shape, F32),
        grid_spec=pltpu.PrefetchScalarGridSpec(
            num_scalar_prefetch=len(scalars),
            grid=(1,),
            in_specs=[hbm] * len(arrays),
            out_specs=out_spec,
            scratch_shapes=scratch,
        ),
        compiler_params=pltpu.CompilerParams(vmem_limit_bytes=LIMIT << 20),
        cost_estimate=pl.CostEstimate(
            flops=products * 6 * B ** 3, bytes_accessed=24 << 20, transcendentals=0
        ),
        name=name,
    )(*scalars, *arrays)


def per_device(density, columns):
    half = lax.axis_index("zh")
    place = lax.axis_index("zl")
    core = lax.axis_index("c")
    local = (lax.axis_index("y") * 4 + lax.axis_index("x")) * 2 + core
    row = half * 32 + local
    starts = (core * PART[1], (1 - core) * PART[0])
    planes = [
        lax.all_gather(
            lax.dynamic_slice_in_dim(density, start, size, axis=0).reshape(size * 2, B, B),
            ("zh", "zl"), axis=0, tiled=True,
        )
        for start, size in zip(starts, PART)
    ]

    forward = [(i, (i + 1) % 64) for i in range(64)]
    backward = [(b, a) for a, b in forward]
    wide = jnp.concatenate(
        [lax.ppermute(columns, ROW, forward), columns, lax.ppermute(columns, ROW, backward)]
    )
    both = lax.all_gather(wide, ("zh", "zl"), axis=1, tiled=True)
    low, high = both[:, :S].reshape(-1), both[:, S:].reshape(-1)
    at_end = (local == 0) | (local == 31)
    cols = jnp.where(half == 0, low, high)
    send_cols = jnp.where((half == 0) ^ at_end, low, high)
    send_half = jnp.where(at_end, 1 - half, half)
    where = jnp.stack(
        [row * ROWS, place, core, send_half, (send_half * 32 + local) * ROWS, half]
    ).astype(jnp.int32)
    lists = plan(where, cols, send_cols)
    planes[0], lists = lax.optimization_barrier((planes[0], lists))
    list0, list1, list2, list3, list4 = (lists[2 * n : 2 * n + 2] for n in range(5))
    counts, sends0, sends1 = lists[10:]

    inner = [(h * 32 + i, h * 32 + (i + 1) % 32) for h in range(2) for i in range(1, 32, 2)]
    inner += [(b, a) for a, b in inner]
    swap = [(0, 1), (1, 0)]
    panel = pltpu.VMEM((ZERO + 1, B, B), F32)
    blocks = pltpu.VMEM((THIRD + 1, B, B), F32)
    hbm = pl.BlockSpec(memory_space=pl.ANY)

    chip0 = lax.ppermute(planes[0], "c", swap)
    far0 = lax.ppermute(pack(0, counts, sends0, planes[0]), ROW, inner)
    square = call(
        first_kernel, (where, counts, *list0), (planes[0], chip0),
        (THIRD, B, B), hbm, [panel, blocks, pltpu.SemaphoreType.DMA((3,))], 400, "first",
    )
    square = call(
        early_kernel, (where, counts, *list1), (planes[0], far0, square),
        (THIRD, B, B), hbm, [panel, blocks, pltpu.SemaphoreType.DMA((4,))], 100, "early",
    )
    planes[1], square = lax.optimization_barrier((planes[1], square))
    chip1 = lax.ppermute(planes[1], "c", swap)
    far1 = lax.ppermute(pack(1, counts, sends1, planes[1]), ROW, inner)
    halves_of = (planes[0], chip0, planes[1], chip1)
    square = call(
        second_kernel, (where, counts, *list2), (*halves_of, far0, square),
        (THIRD, B, B), hbm, [panel, blocks, pltpu.SemaphoreType.DMA((7,))], 400, "second",
    )
    result = call(
        last_kernel, (where, counts, *list3, *list4, cols), (*halves_of, far0, far1, square),
        (ROWS * 2, B, B), pl.BlockSpec((ROWS * 2, B, B), lambda i, *_: (0, 0, 0)),
        [panel, blocks, pltpu.VMEM((ROWS * 2 + 1, B, B), F32), pltpu.SemaphoreType.DMA((7,))], 200, "last",
    )
    return result.reshape(ROWS, 2, B, B)


def solution(mesh):
    fine = Mesh(mesh.devices.reshape(2, 4, 4, 2, 8), ("zh", "y", "x", "c", "zl"))
    return jax.shard_map(
        per_device,
        mesh=fine,
        in_specs=(P(ROW, "zl", None, None), P(ROW, "zl")),
        out_specs=P(ROW, "zl", None, None),
        check_vma=False,
    )
```
